32 devices in a mesh: mat: 4 (over z), pts: 8 (over y, x, core).
Axes of the slice: x: 2, y: 2, z: 4, core: 2. Of those that a mesh axis runs over, the one named last changes fastest.
Arguments:
- basis_values: bfloat16 [128, 2048, 512], P(('mat', 'pts')), may hold values from -6 to 6
- tile_ids: int32 [128, 4], P(('mat', 'pts')), may hold values from 0 to 3, as said below
- density_matrix: bfloat16 [512, 512], P('mat'), may hold values from -0.01171875 to 0.01171875
- descriptors: bfloat16 [128, 2048, 64], P(('mat', 'pts')), may hold values from -6 to 6
- grid_weights: float32 [128, 2048], P(('mat', 'pts')), may hold values from 0.25 to 2
- centre_ids: int32 [128, 2048], P(('mat', 'pts')), may hold values from 0 to 127
- density_scale: float32 [64], replicated, may hold values from -4 to 4
- norm_gain: float32 [64], replicated, may hold values from 0.1 to 1.9
- w_first: bfloat16 [64, 256], replicated, may hold values from -0.75 to 0.75
- b_first: float32 [256], replicated, may hold values from -3 to 3
- w_second: bfloat16 [256, 256], replicated, may hold values from -0.375 to 0.375
- b_second: float32 [256], replicated, may hold values from -3 to 3
- w_third: bfloat16 [256, 64], replicated, may hold values from -0.375 to 0.375
- b_third: float32 [64], replicated, may hold values from -3 to 3
Outputs:
- potential_matrix: bfloat16 [512, 512], P('mat', 'pts')
- centre_features: bfloat16 [128, 64], P('pts')
The draws below stay inside these ranges and needn't reach their ends.
Inputs may be any that keep to these rules, and one draw needn't show every extreme that they name: `tile_ids`: the 4 tiles t of one batch have 4 different values of t.
All inputs are finite; a program needn't handle non-finite values.
Results may differ from the reference program's by a relative error of at most 0.0064.
Values may be sent and summed in bfloat16 or wider, within the bound.
A program may use at most 64 MiB of HBM per device.

```python
import math
import jax
import jax.numpy as jnp
from jax import lax

ORB = 512
TILE = 128
FEAT = 64
HID = 256
PTS = 2048
BATCHES = 128
KT = 4
TPD = 1
NBAS = 512
NT = 4
NCENT = 128


def draw_tile_ids(key, part):
    owner_total = NT // TPD
    leading, trailing = jax.random.split(jax.random.fold_in(key, 11))
    scores = jax.random.randint(leading, (BATCHES, owner_total), 0, 1 << 20) * owner_total + jnp.arange(owner_total, dtype=jnp.int32)[None, :]
    owners = jnp.argsort(scores, axis=1)[:, :KT].astype(jnp.int32)
    local_tiles = jax.random.randint(trailing, (BATCHES, KT), 0, TPD).astype(jnp.int32)
    return (owners * TPD + local_tiles).astype(jnp.int32)


def centre_lists(key):
    return jax.random.randint(jax.random.fold_in(key, 23), (BATCHES, PTS), 0, NCENT).astype(jnp.int32)


def draw_centre_ids(key, part):
    return centre_lists(key)


def draw_descriptors(key, part):
    owners = centre_lists(key)
    spread_key, value_key = jax.random.split(jax.random.fold_in(key, 29))
    log_scales = jax.random.uniform(spread_key, (NCENT, FEAT), jnp.float32, math.log(0.3), math.log(3.0))
    values = jax.random.normal(value_key, (BATCHES, PTS, FEAT), jnp.float32)
    scales = jnp.exp(log_scales)[owners]
    return jnp.clip(scales * values, -6.0, 6.0).astype(jnp.bfloat16)


def level_of(own_key, dims, shards, low, largest):
    loudness, own = 1.0, jax.random.fold_in(own_key, 6)
    for position, parts in shards:
        steps = jnp.exp(jax.random.uniform(jax.random.fold_in(own, position), (parts,), jnp.float32, low / len(shards), largest / len(shards)))
        loudness = loudness * jnp.repeat(steps, dims[position] // parts).reshape([-1 if axis == position else 1 for axis in range(len(dims))])
    return loudness


def scatter_about(rng, dims, width, most, pieces=(), kind=jnp.bfloat16):
    array = width * jax.random.normal(rng, dims, jnp.float32)
    if pieces:
        array = array * level_of(rng, dims, pieces, -0.22, 0.18)
    return jnp.clip(array, -most, most).astype(kind)


def setup_inputs(seed: int = 0) -> dict:
    arg_keys = jax.random.split(jax.random.key(seed), 15)
    basis_values = scatter_about(arg_keys[0], (BATCHES, PTS, ORB), 1.0, 6.0, ((0, 32),))
    tile_ids = draw_tile_ids(jax.random.fold_in(arg_keys[14], 71), 0)
    density_matrix = scatter_about(arg_keys[2], (NBAS, NBAS), (ORB * ORB) ** -0.5, 0.01171875, ((0, 4),))
    descriptors = draw_descriptors(jax.random.fold_in(arg_keys[14], 71), 0)
    grid_weights = jnp.clip(jnp.exp(math.log(2.0) - 2.0794415 * jax.random.uniform(arg_keys[4], (BATCHES, PTS), jnp.float32) ** level_of(arg_keys[4], (BATCHES, PTS), ((0, 32),), -0.2, 0.2)), 0.25, 2.0)
    centre_ids = draw_centre_ids(jax.random.fold_in(arg_keys[14], 71), 0)
    density_scale = scatter_about(arg_keys[6], (FEAT,), 1.0, 4.0, (), jnp.float32)
    norm_gain = jnp.clip(1.0 + 0.18 * jax.random.normal(arg_keys[7], (FEAT,), jnp.float32), 0.1, 1.9)
    w_first = scatter_about(arg_keys[8], (FEAT, HID), FEAT ** -0.5, 0.75)
    b_first = scatter_about(arg_keys[9], (HID,), 0.5, 3.0, (), jnp.float32)
    w_second = scatter_about(arg_keys[10], (HID, HID), HID ** -0.5, 0.375)
    b_second = scatter_about(arg_keys[11], (HID,), 0.5, 3.0, (), jnp.float32)
    w_third = scatter_about(arg_keys[12], (HID, FEAT), HID ** -0.5, 0.375)
    b_third = scatter_about(arg_keys[13], (FEAT,), 0.5, 3.0, (), jnp.float32)
    return {"basis_values": basis_values, "tile_ids": tile_ids, "density_matrix": density_matrix, "descriptors": descriptors, "grid_weights": grid_weights, "centre_ids": centre_ids, "density_scale": density_scale, "norm_gain": norm_gain, "w_first": w_first, "b_first": b_first, "w_second": w_second, "b_second": b_second, "w_third": w_third, "b_third": b_third}


def orbital_rows(tile_list):
    offsets = jnp.arange(TILE, dtype=jnp.int32)
    return (tile_list.astype(jnp.int32)[:, None] * TILE + offsets[None, :]).reshape(-1).astype(jnp.int32)

def centre_network(summed, norm_gain, w_first, b_first, w_second, b_second, w_third, b_third):
    inverse = lax.rsqrt(lax.optimization_barrier(jnp.mean(summed * summed, axis=1, keepdims=True)) + 1e-05)
    normed = (summed * inverse * norm_gain).astype(jnp.bfloat16)
    hidden_one = jax.nn.silu(jnp.dot(normed, w_first, preferred_element_type=jnp.float32) + b_first).astype(jnp.bfloat16)
    hidden_two = jax.nn.silu(jnp.dot(hidden_one, w_second, preferred_element_type=jnp.float32) + b_second).astype(jnp.bfloat16)
    return (jnp.dot(hidden_two, w_third, preferred_element_type=jnp.float32) + b_third).astype(jnp.bfloat16)

def reference(basis_values, tile_ids, density_matrix, descriptors, grid_weights, centre_ids, density_scale, norm_gain, w_first, b_first, w_second, b_second, w_third, b_third):

    def batch_density(inputs):
        values, tile_list = inputs
        orbital = orbital_rows(tile_list)
        panel_full = density_matrix[orbital][:, orbital]
        projected = jnp.dot(values, panel_full, preferred_element_type=jnp.float32)
        return lax.optimization_barrier(jnp.sum(values.astype(jnp.float32) * projected, axis=1))
    density = lax.map(batch_density, (basis_values, tile_ids))
    radial_terms = descriptors.astype(jnp.float32)
    features = jax.nn.silu(density[:, :, None] * density_scale + radial_terms)
    weighted_feat = grid_weights[:, :, None] * features
    centre_sum = jax.ops.segment_sum(weighted_feat.reshape(-1, FEAT), centre_ids.reshape(-1), num_segments=NCENT)
    centre_features = centre_network(centre_sum, norm_gain, w_first, b_first, w_second, b_second, w_third, b_third)
    nearest = centre_features[centre_ids].astype(jnp.float32)
    factor = NT / (KT * math.sqrt(PTS * FEAT * BATCHES))
    point_potential = grid_weights * density * lax.optimization_barrier(jnp.sum(nearest * radial_terms, axis=2)) * factor

    def assemble(accumulated, inputs):
        values, tile_list, local_potential = inputs
        orbital = orbital_rows(tile_list)
        weighted = (local_potential[:, None] * values.astype(jnp.float32)).astype(jnp.bfloat16)
        tile_block = jnp.dot(values.T, weighted, preferred_element_type=jnp.float32)
        return (accumulated.at[orbital[:, None], orbital[None, :]].add(tile_block), None)
    accumulated, ignored = lax.scan(assemble, jnp.zeros((NBAS, NBAS), jnp.float32), (basis_values, tile_ids, point_potential))
    return (accumulated.astype(jnp.bfloat16), centre_features)
```

```python
import functools
import math

import jax
import jax.numpy as jnp
from jax import lax
from jax.experimental import pallas as pl
from jax.experimental.pallas import tpu as pltpu
from jax.sharding import PartitionSpec as P

CHUNK = 512
SPLIT = 2
MESH = pl.DeviceIdType.MESH
F32 = jnp.float32
BF16 = jnp.bfloat16
NT_DIMS = (((1,), (1,)), ((), ()))


def silu(v):
    h = 0.5 * v
    return h + h * jnp.tanh(h)


def place(pot, cf, out_pot, out_cf):
    out_pot[...] = pot[...]
    out_cf[...] = cf[...]


def kernel(
    nm, npts, factor,
    v_hbm, d_hbm, tiles_hbm, dm_hbm, gw_hbm, ids_hbm, scale_hbm, gain_hbm,
    w1_hbm, b1_hbm, w2_hbm, b2_hbm, w3_hbm, b3_hbm,
    out_pot, out_cf,
    tiles, dm, gw, ids, scale, gain, w1, b1, w2, b2, w3, b3,
    vbuf, dbuf, vt, oh, dens, pps, panel, cpart, cs_src, cs_in, cz_src, cz_in,
    full, cf_s, cft, acc, snd, rin, red, zsnd, zin,
    isem, vsem, dsem, ag_s, ag_r, fw_s, fw_r, cs_s, cs_r, cz_s, cz_r, cg_s, cg_r, rp_s, rp_r, rz_s, rz_r,
):
    m = lax.axis_index("mat")
    p = lax.axis_index("pts")
    batches = len(vbuf)
    per_batch, points, tile = vbuf[0].shape
    rows, nb = dm.shape
    ntile = nb // tile
    feat = dbuf.shape[1]
    ncent = oh.shape[1]
    per = points // CHUNK
    slab = nb // npts
    piece = rows // SPLIT

    small = [
        pltpu.make_async_copy(a, b, isem.at[i]) for i, (a, b) in enumerate((
            (tiles_hbm, tiles), (dm_hbm, dm), (ids_hbm, ids), (gw_hbm, gw), (scale_hbm, scale), (gain_hbm, gain),
            (w1_hbm, w1), (b1_hbm, b1), (w2_hbm, w2), (b2_hbm, b2), (w3_hbm, w3), (b3_hbm, b3)))]

    def vcopy(b, j):
        return pltpu.make_async_copy(v_hbm.at[b, :, pl.ds(j * tile, tile)], vbuf[b].at[j], vsem.at[b, j])

    def dcopy(b):
        return pltpu.make_async_copy(d_hbm.at[b], dbuf.at[b], dsem.at[b])

    barrier = pltpu.get_barrier_semaphore()
    for k in range(1, npts):
        pl.semaphore_signal(barrier, inc=1, device_id={"pts": lax.rem(p + k, npts)}, device_id_type=MESH)
    for k in range(1, nm):
        pl.semaphore_signal(barrier, inc=1, device_id={"mat": lax.rem(m + k, nm)}, device_id_type=MESH)
    for c in small[:3]:
        c.start()
    for j in range(per_batch):
        vcopy(0, j).start()
    for c in small[3:]:
        c.start()
    for b in range(1, batches):
        for j in range(per_batch):
            vcopy(b, j).start()
    for b in range(batches):
        dcopy(b).start()
    for c in small[:3]:
        c.wait()
    pl.semaphore_wait(barrier, npts + nm - 2)

    def remote(src, dst, s, r, **where):
        return pltpu.make_async_remote_copy(
            src_ref=src, dst_ref=dst, send_sem=s, recv_sem=r, device_id=where, device_id_type=MESH
        )

    def at_rows(owner, part):
        return pl.ds(pl.multiple_of(owner * rows + part * piece, piece), piece)

    g = lax.rem(p, SPLIT)
    base = p - g
    peer = [lax.rem(m + k, nm) for k in range(nm)]
    near = m + 1 - 2 * lax.rem(m, 2)
    order = [near] + [lax.rem(m + 2 * (k // 2) + lax.rem(m + k, 2) - lax.rem(m, 2) + nm, nm) for k in range(2, nm)]
    ag = []
    for k, to in enumerate(order):
        ag.append(remote(
            dm.at[pl.ds(pl.multiple_of(g * piece, piece), piece)], panel.at[at_rows(m, g)],
            ag_s.at[to], ag_r.at[m], mat=to))
    for c in ag:
        c.start()
    panel[pl.ds(pl.multiple_of(m * rows, rows), rows), :] = dm[...]

    def prepare(b):
        for j in range(per_batch):
            vcopy(b, j).wait()
        held = [tiles[b, j] for j in range(per_batch)]

        def find(t, value, otherwise):
            for j in range(per_batch):
                otherwise = jnp.where(held[j] == t, value(j), otherwise)
            return otherwise

        spot = [find(t, lambda j: j, 0) for t in range(ntile)]
        here = [find(t, lambda j: 1, 0) for t in range(ntile)]

        def body(i, carry):
            at = pl.ds(pl.multiple_of(i * CHUNK, CHUNK), CHUNK)
            for t in range(ntile):
                x = vbuf[b][spot[t], at, :]
                if ntile != per_batch:
                    x = jnp.where(here[t] == 1, x, jnp.zeros_like(x))
                vt[b, t * tile:(t + 1) * tile, at] = x.T
            which = lax.broadcasted_iota(jnp.int32, (ncent, CHUNK), 0)
            oh[b, :, at] = jnp.where(which == ids[b:b + 1, at], 1.0, 0.0).astype(BF16)
            return carry

        lax.fori_loop(0, per, body, 0)

    for b in range(batches):
        prepare(b)
    for c in small[3:]:
        c.wait()

    scale_col = jnp.broadcast_to(scale[...], (128, feat)).T[:, :1]
    cpart[...] = jnp.zeros_like(cpart)

    fw = []

    def receive(k):
        src = order[k]
        remote(dm.at[pl.ds(0, piece)], panel.at[at_rows(src, g)], ag_s.at[src], ag_r.at[src], mat=src).wait_recv()
        held = panel.at[at_rows(src, g)]
        mine = []
        for s in range(1, SPLIT):
            i = k * (SPLIT - 1) + s - 1
            c = remote(held, held, fw_s.at[i], fw_r.at[i], pts=base + lax.rem(g + s, SPLIT))
            c.start()
            mine.append(c)
        fw.extend(mine)
        return mine

    def part(b, pair):
        at = pl.ds(pl.multiple_of(pair * 2 * rows, 2 * rows), 2 * rows)
        q = jnp.dot(panel[at, :], vt[b], preferred_element_type=F32)
        return jnp.sum(q * vt[b, at, :].astype(F32), axis=0, keepdims=True)

    pairs = nm // 2
    own = m // 2
    for c in receive(0):
        c.wait_recv()

    def first(b, carry):
        dens[b] = part(b, own)
        return carry

    lax.fori_loop(0, batches, first, 0)
    for k in range(1, nm - 1):
        receive(k)
    for c in fw[SPLIT - 1:]:
        c.wait_recv()

    def second(b, carry):
        d = dens[b]
        for k in range(1, pairs):
            d = d + part(b, lax.rem(own + k, pairs))
        dens[b] = d
        dcopy(b).wait()
        wf = gw[pl.ds(b, 1), :] * silu(d * scale_col + dbuf[b].astype(F32))
        high = wf.astype(BF16)
        low = (wf - high.astype(F32)).astype(BF16)
        both = lax.dot_general(
            jnp.concatenate([high, low], axis=0), oh[b], NT_DIMS, preferred_element_type=F32)
        cpart[...] += both[:feat] + both[feat:]
        return carry

    lax.fori_loop(0, batches, second, 0)

    fp = feat // npts
    for i in range(npts):
        cs_src[i] = cpart[i * fp:(i + 1) * fp, :]
    cs = []
    for k in range(1, npts):
        to = lax.rem(p + k, npts)
        c = remote(cs_src.at[to], cs_in.at[k - 1], cs_s.at[k - 1], cs_r.at[k - 1], pts=to)
        c.start()
        cs.append(c)
    mine = cs_src[p]
    for k in range(1, npts):
        cs[k - 1].wait_recv()
        mine = mine + cs_in[k - 1]
    cz_src[...] = mine
    cz = []
    for k in range(1, nm):
        c = remote(cz_src, cz_in.at[m], cz_s.at[k - 1], cz_r.at[k - 1], mat=lax.rem(m + k, nm))
        c.start()
        cz.append(c)
    cz_in[m] = mine
    for c in cz:
        c.wait_recv()
    total = cz_in[0]
    for i in range(1, nm):
        total = total + cz_in[i]
    full[p] = total
    cg = []
    for k in range(1, npts):
        c = remote(full.at[p], full.at[p], cg_s.at[k - 1], cg_r.at[k - 1], pts=lax.rem(p + k, npts))
        c.start()
        cg.append(c)
    for c in cg:
        c.wait_recv()

    summed = jnp.concatenate([full[i] for i in range(npts)], axis=0).T
    inverse = lax.rsqrt(jnp.mean(summed * summed, axis=1, keepdims=True) + 1e-05)
    normed = (summed * inverse * gain[...]).astype(BF16)
    one = silu(jnp.dot(normed, w1[...], preferred_element_type=F32) + b1[...]).astype(BF16)
    two = silu(jnp.dot(one, w2[...], preferred_element_type=F32) + b2[...]).astype(BF16)
    cf = (lax.dot_general(two, w3[...], NT_DIMS, preferred_element_type=F32) + b3[...]).astype(BF16).astype(F32)
    cf_s[...] = cf
    cft[...] = cf.T.astype(BF16)
    cent = out_cf.shape[0]
    out_cf[...] = cf_s[pl.ds(pl.multiple_of(p * cent, cent), cent), :].astype(BF16)

    group = [[t for t in range(ntile) if (t + t // 2) % 2 == s] for s in range(2)]
    per_tile = tile // slab
    owners = [[t * per_tile + i for t in group[s] for i in range(per_tile)] for s in range(2)]
    width = nb // nm
    half = nb // 2
    acc[...] = jnp.zeros_like(acc)

    def side(b, s):
        return jnp.concatenate([vt[b, t * tile:(t + 1) * tile, :] for t in group[s]], axis=0)

    def block0(b, carry):
        nearest = jnp.dot(cft[...], oh[b], preferred_element_type=F32)
        along = jnp.sum(nearest * dbuf[b].astype(F32), axis=0, keepdims=True)
        pp = gw[pl.ds(b, 1), :] * dens[b] * along * factor
        pps[b] = pp
        w = (side(b, 0).astype(F32) * pp).astype(BF16)
        r = lax.dot_general(w, side(b, 0), NT_DIMS, preferred_element_type=F32)
        for i, o in enumerate(owners[0]):
            acc[o, 0] += r[i * slab:(i + 1) * slab]
        r = lax.dot_general(w, side(b, 1), NT_DIMS, preferred_element_type=F32)
        for i, o in enumerate(owners[0]):
            acc[o, 1] += r[i * slab:(i + 1) * slab]
        return carry

    def block1(b, carry):
        x = side(b, 1)
        w = (x.astype(F32) * pps[b]).astype(BF16)
        r = lax.dot_general(w, x, NT_DIMS, preferred_element_type=F32)
        for i, o in enumerate(owners[1]):
            acc[o, 1] += r[i * slab:(i + 1) * slab]
        return carry

    def send(to, s):
        c = remote(snd.at[to, s], rin.at[p, s], rp_s.at[to, s], rp_r.at[p, s], pts=to)

        @pl.when(to != p)
        def _():
            c.start()

    lax.fori_loop(0, batches, block0, 0)
    for o in owners[0]:
        snd[o, 0] = acc[o, 0].astype(BF16)
        snd[o, 1] = acc[o, 1].astype(BF16)
    across = jnp.concatenate([acc[o, 1] for o in owners[0]], axis=0).T
    for i, o in enumerate(owners[1]):
        acc[o, 0] = across[i * slab:(i + 1) * slab]
        snd[o, 0] = across[i * slab:(i + 1) * slab].astype(BF16)
    for o in range(npts):
        send(o, 0)
        if o in owners[0]:
            send(o, 1)
    lax.fori_loop(0, batches, block1, 0)
    for o in owners[1]:
        snd[o, 1] = acc[o, 1].astype(BF16)
        send(o, 1)
    for s in range(2):
        mine = acc[p, s]
        for k in range(1, npts):
            src = lax.rem(p + k, npts)
            remote(snd.at[src, s], rin.at[src, s], rp_s.at[src, s], rp_r.at[src, s], pts=src).wait_recv()
            mine = mine + rin[src, s].astype(F32)
        for i, t in enumerate(group[s]):
            red[t] = mine[:, i * tile:(i + 1) * tile]
            zsnd[t] = mine[:, i * tile:(i + 1) * tile].astype(BF16)
    rz = []
    for k in range(1, nm):
        to = lax.rem(m + k, nm)
        c = remote(zsnd.at[to], zin.at[k - 1], rz_s.at[k - 1], rz_r.at[k - 1], mat=to)
        c.start()
        rz.append(c)
    mine = red[m]
    for k in range(1, nm):
        rz[k - 1].wait_recv()
        mine = mine + zin[k - 1].astype(F32)
    out_pot[...] = mine.astype(BF16)

    for c in ag + fw + cs + cz + cg + rz:
        c.wait_send()
    for to in range(npts):
        for s in range(2):
            c = remote(snd.at[to, s], rin.at[p, s], rp_s.at[to, s], rp_r.at[p, s], pts=to)

            @pl.when(to != p)
            def _():
                c.wait_send()


def shards(
    nm, npts,
    basis_values, tile_ids, density_matrix, descriptors, grid_weights, centre_ids,
    density_scale, norm_gain, w_first, b_first, w_second, b_second, w_third, b_third,
):
    batches, points, orbitals = basis_values.shape
    per_batch = tile_ids.shape[1]
    tile = orbitals // per_batch
    rows, nb = density_matrix.shape
    feat = descriptors.shape[2]
    hid = w_first.shape[1]
    ntile = nb // tile
    cent = 16
    ncent = cent * npts
    slab = nb // npts
    width = nb // nm
    factor = ntile / (per_batch * math.sqrt(points * feat * batches * nm * npts))
    vm = pl.BlockSpec(memory_space=pltpu.VMEM)
    anyw = pl.BlockSpec(memory_space=pl.ANY)
    fp = feat // npts
    dma = pltpu.SemaphoreType.DMA
    nfw = (nm - 1) * (SPLIT - 1)
    potential, centre_features = pl.pallas_call(
        functools.partial(kernel, nm, npts, factor),
        out_shape=(
            jax.ShapeDtypeStruct((slab, width), BF16),
            jax.ShapeDtypeStruct((cent, feat), BF16),
        ),
        in_specs=[anyw] * 14,
        out_specs=(vm, vm),
        scratch_shapes=[
            pltpu.SMEM((batches, per_batch), jnp.int32),
            pltpu.VMEM((rows, nb), BF16),
            pltpu.VMEM((batches, points), F32),
            pltpu.VMEM((batches, points), jnp.int32),
            pltpu.VMEM((1, feat), F32),
            pltpu.VMEM((1, feat), F32),
            pltpu.VMEM((feat, hid), BF16),
            pltpu.VMEM((1, hid), F32),
            pltpu.VMEM((hid, hid), BF16),
            pltpu.VMEM((1, hid), F32),
            pltpu.VMEM((feat, hid), BF16),
            pltpu.VMEM((1, feat), F32),
            [pltpu.VMEM((per_batch, points, tile), BF16) for _ in range(batches)],
            pltpu.VMEM((batches, feat, points), BF16),
            pltpu.VMEM((batches, nb, points), BF16),
            pltpu.VMEM((batches, ncent, points), BF16),
            pltpu.VMEM((batches, 1, points), F32),
            pltpu.VMEM((batches, 1, points), F32),
            pltpu.VMEM((nb, nb), BF16),
            pltpu.VMEM((feat, ncent), F32),
            pltpu.VMEM((npts, fp, ncent), F32),
            pltpu.VMEM((npts, fp, ncent), F32),
            pltpu.VMEM((fp, ncent), F32),
            pltpu.VMEM((nm, fp, ncent), F32),
            pltpu.VMEM((npts, fp, ncent), F32),
            pltpu.VMEM((ncent, feat), F32),
            pltpu.VMEM((feat, ncent), BF16),
            pltpu.VMEM((npts, 2, slab, nb // 2), F32),
            pltpu.VMEM((npts, 2, slab, nb // 2), BF16),
            pltpu.VMEM((npts, 2, slab, nb // 2), BF16),
            pltpu.VMEM((nm, slab, width), F32),
            pltpu.VMEM((nm, slab, width), BF16),
            pltpu.VMEM((nm, slab, width), BF16),
            dma((12,)), dma((batches, per_batch)), dma((batches,)),
            dma((nm,)), dma((nm,)),
            dma((nfw,)), dma((nfw,)),
            dma((npts - 1,)), dma((npts - 1,)),
            dma((nm - 1,)), dma((nm - 1,)),
            dma((npts - 1,)), dma((npts - 1,)),
            dma((npts, 2)), dma((npts, 2)),
            dma((nm - 1,)), dma((nm - 1,)),
        ],
        compiler_params=pltpu.CompilerParams(
            collective_id=0, has_side_effects=True, vmem_limit_bytes=60 * 1024 * 1024
        ),
    )(
        basis_values, descriptors.transpose(0, 2, 1), tile_ids, density_matrix, grid_weights, centre_ids,
        density_scale.reshape(1, -1), norm_gain.reshape(1, -1),
        w_first, b_first.reshape(1, -1), w_second, b_second.reshape(1, -1),
        w_third.T, b_third.reshape(1, -1),
    )
    potential, centre_features = pl.pallas_call(
        place,
        out_shape=(
            jax.ShapeDtypeStruct((slab, width), BF16),
            jax.ShapeDtypeStruct((cent, feat), BF16),
        ),
        in_specs=[vm, vm],
        out_specs=(vm, vm),
    )(potential, centre_features)
    return (potential.T, centre_features)


def solution(mesh):
    return jax.shard_map(
        functools.partial(shards, mesh.shape["mat"], mesh.shape["pts"]),
        mesh=mesh,
        in_specs=(
            P(("mat", "pts"), None, None),
            P(("mat", "pts"), None),
            P("mat", None),
            P(("mat", "pts"), None, None),
            P(("mat", "pts"), None),
            P(("mat", "pts"), None),
            P(), P(), P(), P(), P(), P(), P(), P(),
        ),
        out_specs=(P("mat", "pts"), P("pts", None)),
        check_vma=False,
    )
```

```python
import functools
import math

import jax
import jax.numpy as jnp
from jax import lax
from jax.experimental import pallas as pl
from jax.experimental.pallas import tpu as pltpu
from jax.sharding import PartitionSpec as P

CHUNK = 512
SPLIT = 2
MESH = pl.DeviceIdType.MESH
F32 = jnp.float32
BF16 = jnp.bfloat16
NT_DIMS = (((1,), (1,)), ((), ()))


def silu(v):
    h = 0.5 * v
    return h + h * jnp.tanh(h)


def place(pot, cf, out_pot, out_cf):
    out_pot[...] = pot[...]
    out_cf[...] = cf[...]


def kernel(
    nm, npts, factor,
    v_hbm, d_hbm, tiles_hbm, dm_hbm, gw_hbm, ids_hbm, scale_hbm, gain_hbm,
    w1_hbm, b1_hbm, w2_hbm, b2_hbm, w3_hbm, b3_hbm,
    out_pot, out_cf,
    tiles, gw, ids, scale, gain, w1, b1, w2, b2, w3, b3,
    vbuf, dbuf, vt, oh, dens, pps, panel, cpart, cs_src, cs_in, cz_src, cz_in,
    full, cf_s, cft, acc, psnd, pin, whole, snd, rin, red, zsnd, zin,
    isem, vsem, dsem, ag_s, ag_r, fw_s, fw_r, cs_s, cs_r, cz_s, cz_r, cg_s, cg_r, pr_s, pr_r, rp_s, rp_r, rz_s, rz_r,
):
    m = lax.axis_index("mat")
    p = lax.axis_index("pts")
    batches = len(vbuf)
    per_batch, points, tile = vbuf[0].shape
    rows, nb = dm_hbm.shape
    ntile = nb // tile
    feat = dbuf.shape[1]
    ncent = oh.shape[1]
    per = points // CHUNK
    slab = nb // npts
    piece = rows // SPLIT

    small = [
        pltpu.make_async_copy(a, b, isem.at[i]) for i, (a, b) in enumerate((
            (tiles_hbm, tiles), (ids_hbm, ids), (dm_hbm, panel.at[pl.ds(pl.multiple_of(m * rows, rows), rows)]),
            (gw_hbm, gw), (scale_hbm, scale), (gain_hbm, gain),
            (w1_hbm, w1), (b1_hbm, b1), (w2_hbm, w2), (b2_hbm, b2), (w3_hbm, w3), (b3_hbm, b3)))]

    def vcopy(b, j):
        return pltpu.make_async_copy(v_hbm.at[b, :, pl.ds(j * tile, tile)], vbuf[b].at[j], vsem.at[b, j])

    def dcopy(b):
        return pltpu.make_async_copy(d_hbm.at[b], dbuf.at[b], dsem.at[b])

    barrier = pltpu.get_barrier_semaphore()
    for k in range(1, npts):
        pl.semaphore_signal(barrier, inc=1, device_id={"pts": lax.rem(p + k, npts)}, device_id_type=MESH)
    for k in range(1, nm):
        pl.semaphore_signal(barrier, inc=1, device_id={"mat": lax.rem(m + k, nm)}, device_id_type=MESH)
    small[0].start()
    for j in range(per_batch):
        vcopy(0, j).start()
    pl.semaphore_wait(barrier, npts + nm - 2)

    def remote(src, dst, s, r, **where):
        return pltpu.make_async_remote_copy(
            src_ref=src, dst_ref=dst, send_sem=s, recv_sem=r, device_id=where, device_id_type=MESH
        )

    def at_rows(owner, part):
        return pl.ds(pl.multiple_of(owner * rows + part * piece, piece), piece)

    g = lax.rem(p, SPLIT)
    base = p - g
    near = m + 1 - 2 * lax.rem(m, 2)
    order = [near] + [lax.rem(m + 2 * (k // 2) + lax.rem(m + k, 2) - lax.rem(m, 2) + nm, nm) for k in range(2, nm)]
    ag = []
    for k, to in enumerate(order):
        ag.append(remote(
            dm_hbm.at[pl.ds(pl.multiple_of(g * piece, piece), piece)], panel.at[at_rows(m, g)],
            ag_s.at[to], ag_r.at[m], mat=to))
    for c in ag:
        c.start()
    for c in small[1:3]:
        c.start()
    for b in range(1, batches):
        for j in range(per_batch):
            vcopy(b, j).start()
    for c in small[3:]:
        c.start()
    for b in range(batches):
        dcopy(b).start()
    small[0].wait()
    small[1].wait()
    small[2].wait()

    def prepare(b):
        for j in range(per_batch):
            vcopy(b, j).wait()
        held = [tiles[b, j] for j in range(per_batch)]

        def find(t, value, otherwise):
            for j in range(per_batch):
                otherwise = jnp.where(held[j] == t, value(j), otherwise)
            return otherwise

        spot = [find(t, lambda j: j, 0) for t in range(ntile)]
        here = [find(t, lambda j: 1, 0) for t in range(ntile)]

        def body(i, carry):
            at = pl.ds(pl.multiple_of(i * CHUNK, CHUNK), CHUNK)
            for t in range(ntile):
                x = vbuf[b][spot[t], at, :]
                if ntile != per_batch:
                    x = jnp.where(here[t] == 1, x, jnp.zeros_like(x))
                vt[b, t * tile:(t + 1) * tile, at] = x.T
            which = lax.broadcasted_iota(jnp.int32, (ncent, CHUNK), 0)
            oh[b, :, at] = jnp.where(which == ids[b:b + 1, at], 1.0, 0.0).astype(BF16)
            return carry

        lax.fori_loop(0, per, body, 0)

    for b in range(batches):
        prepare(b)
    for c in small[3:]:
        c.wait()

    scale_col = jnp.broadcast_to(scale[...], (128, feat)).T[:, :1]
    cpart[...] = jnp.zeros_like(cpart)

    fw = []

    def receive(k):
        src = order[k]
        remote(dm_hbm.at[pl.ds(0, piece)], panel.at[at_rows(src, g)], ag_s.at[src], ag_r.at[src], mat=src).wait_recv()
        held = panel.at[at_rows(src, g)]
        mine = []
        for s in range(1, SPLIT):
            i = k * (SPLIT - 1) + s - 1
            c = remote(held, held, fw_s.at[i], fw_r.at[i], pts=base + lax.rem(g + s, SPLIT))
            c.start()
            mine.append(c)
        fw.extend(mine)
        return mine

    def part(b, owner):
        at = pl.ds(pl.multiple_of(owner * rows, rows), rows)
        q = jnp.dot(panel[at, :], vt[b], preferred_element_type=F32)
        return jnp.sum(q * vt[b, at, :].astype(F32), axis=0, keepdims=True)

    passing = receive(0)
    for b in range(batches):
        dens[b] = part(b, m)
    for k in range(nm - 2):
        for c in passing:
            c.wait_recv()
        passing = receive(k + 1)
        for b in range(batches):
            dens[b] += part(b, order[k])
    for c in passing:
        c.wait_recv()
    for b in range(batches):
        d = dens[b] + part(b, order[nm - 2])
        dens[b] = d
        dcopy(b).wait()
        wf = gw[pl.ds(b, 1), :] * silu(d * scale_col + dbuf[b].astype(F32))
        high = wf.astype(BF16)
        low = (wf - high.astype(F32)).astype(BF16)
        both = lax.dot_general(
            jnp.concatenate([high, low], axis=0), oh[b], NT_DIMS, preferred_element_type=F32)
        cpart[...] += both[:feat] + both[feat:]

    around = [lax.rem(p + k, npts) for k in sorted(range(1, npts), key=lambda k: -min(k, npts - k))]
    fp = feat // npts
    for i in range(npts):
        cs_src[i] = cpart[i * fp:(i + 1) * fp, :]
    cs = []
    for to in around:
        c = remote(cs_src.at[to], cs_in.at[p], cs_s.at[to], cs_r.at[p], pts=to)
        c.start()
        cs.append(c)
    mine = cs_src[p]
    for src in around[::-1]:
        remote(cs_src.at[src], cs_in.at[src], cs_s.at[src], cs_r.at[src], pts=src).wait_recv()
        mine = mine + cs_in[src]
    cz_src[...] = mine
    cz = []
    for k, to in enumerate(order[::-1]):
        c = remote(cz_src, cz_in.at[m], cz_s.at[k], cz_r.at[k], mat=to)
        c.start()
        cz.append(c)
    cz_in[m] = mine
    for c in cz:
        c.wait_recv()
    total = cz_in[0]
    for i in range(1, nm):
        total = total + cz_in[i]
    full[p] = total
    cg = []
    for to in around:
        c = remote(full.at[p], full.at[p], cg_s.at[to], cg_r.at[p], pts=to)
        c.start()
        cg.append(c)
    for src in around[::-1]:
        remote(full.at[src], full.at[src], cg_s.at[src], cg_r.at[src], pts=src).wait_recv()

    summed = jnp.concatenate([full[i] for i in range(npts)], axis=0).T
    inverse = lax.rsqrt(jnp.mean(summed * summed, axis=1, keepdims=True) + 1e-05)
    normed = (summed * inverse * gain[...]).astype(BF16)
    one = silu(jnp.dot(normed, w1[...], preferred_element_type=F32) + b1[...]).astype(BF16)
    two = silu(jnp.dot(one, w2[...], preferred_element_type=F32) + b2[...]).astype(BF16)
    cf = (lax.dot_general(two, w3[...], NT_DIMS, preferred_element_type=F32) + b3[...]).astype(BF16).astype(F32)
    cf_s[...] = cf
    cft[...] = cf.T.astype(BF16)
    cent = out_cf.shape[0]
    out_cf[...] = cf_s[pl.ds(pl.multiple_of(p * cent, cent), cent), :].astype(BF16)

    def spot(u, i):
        return 2 * i + (i + u) % 2 if isinstance(u, int) else 2 * i + lax.rem(i + u, 2)

    pairs = npts // 2
    mid = pairs // 2
    core = lax.rem(p, 2)
    chip = p // 2
    buddy = p + 1 - 2 * core

    for b in range(batches):
        nearest = jnp.dot(cft[...], oh[b], preferred_element_type=F32)
        along = jnp.sum(nearest * dbuf[b].astype(F32), axis=0, keepdims=True)
        pps[b] = gw[pl.ds(b, 1), :] * dens[b] * along * factor

    def side(b, u):
        return jnp.concatenate([
            vt[b, pl.ds(pl.multiple_of(spot(u, i) * tile, tile), tile), :] for i in range(mid)], axis=0)

    def quarter(u, w):
        r = 0
        for b in range(batches):
            left = (side(b, u).astype(F32) * pps[b]).astype(BF16)
            r = r + lax.dot_general(left, side(b, w), NT_DIMS, preferred_element_type=F32)
        return r

    def keep(r, first):
        for i in range(mid):
            for q in range(2):
                acc[q, first + i] = r[(2 * i + q) * slab:(2 * i + q + 1) * slab]

    stages = [
        (0, [(spot(0, i), 1) for i in range(mid)] + [(spot(1, i), 0) for i in range(mid)]),
        (2 * mid, [(spot(0, i), 0) for i in range(mid)]),
        (3 * mid, [(spot(1, i), 1) for i in range(mid)]),
    ]

    def pair(n):
        first, entries = stages[n]
        at = pl.ds(first, len(entries))
        return remote(psnd.at[at], pin.at[at], pr_s.at[n], pr_r.at[n], pts=buddy)

    def give(n):
        first, entries = stages[n]
        for e in range(first, first + len(entries)):
            psnd[e] = acc[1 - core, e].astype(BF16)
        pair(n).start()

    def plane(to, u):
        return remote(snd.at[to, u], rin.at[chip, u], rp_s.at[to, u], rp_r.at[chip, u], pts=2 * to + core)

    def spread(n):
        first, entries = stages[n]
        pair(n).wait_recv()
        for e, (to, u) in enumerate(entries):
            both = acc[core, first + e] + pin[first + e].astype(F32)
            whole[to, u] = both
            snd[to, u] = both.astype(BF16)
        for to, u in entries:
            @pl.when(to != chip)
            def _():
                plane(to, u).start()


    def turn(n, carry):
        keep(quarter(n // 2, jnp.where(n == 1, 0, 1)), jnp.where(n == 0, 0, (n + 1) * mid))

        @pl.when(n == 0)
        def _():
            across = jnp.concatenate([acc[q, i] for i in range(mid) for q in range(2)], axis=0)
            keep(across.T, mid)
            give(0)

        @pl.when(n == 1)
        def _():
            spread(0)
            give(1)

        @pl.when(n == 2)
        def _():
            give(2)
            spread(1)

        return carry

    lax.fori_loop(0, 3, turn, 0)
    spread(2)
    early = lax.rem(chip + chip // 2 + 1, 2)
    for n in range(2):
        u = early if n == 0 else 1 - early
        mine = whole[chip, u]
        for k in range(1, pairs):
            src = lax.rem(chip + k, pairs)
            remote(snd.at[src, u], rin.at[src, u], rp_s.at[src, u], rp_r.at[src, u], pts=2 * src + core).wait_recv()
            mine = mine + rin[src, u].astype(F32)
        for i in range(mid):
            to = 2 * i + lax.rem(i + u, 2)
            red[to] = mine[:, i * tile:(i + 1) * tile]
            zsnd[to] = mine[:, i * tile:(i + 1) * tile].astype(BF16)

            @pl.when(to != m)
            def _():
                remote(zsnd.at[to], zin.at[m], rz_s.at[to], rz_r.at[m], mat=to).start()
    mine = red[m]
    for k in range(1, nm):
        src = lax.rem(m + k, nm)
        remote(zsnd.at[src], zin.at[src], rz_s.at[src], rz_r.at[src], mat=src).wait_recv()
        mine = mine + zin[src].astype(F32)
    out_pot[...] = mine.astype(BF16)

    for c in ag + fw + cs + cz + cg:
        c.wait_send()
    for n in range(len(stages)):
        pair(n).wait_send()
    for to in range(pairs):
        for u in range(2):
            @pl.when(to != chip)
            def _():
                plane(to, u).wait_send()
    for k in range(1, nm):
        to = lax.rem(m + k, nm)
        remote(zsnd.at[to], zin.at[m], rz_s.at[to], rz_r.at[m], mat=to).wait_send()


def shards(
    nm, npts,
    basis_values, tile_ids, density_matrix, descriptors, grid_weights, centre_ids,
    density_scale, norm_gain, w_first, b_first, w_second, b_second, w_third, b_third,
):
    batches, points, orbitals = basis_values.shape
    per_batch = tile_ids.shape[1]
    tile = orbitals // per_batch
    rows, nb = density_matrix.shape
    feat = descriptors.shape[2]
    hid = w_first.shape[1]
    ntile = nb // tile
    cent = 16
    ncent = cent * npts
    slab = nb // npts
    width = nb // nm
    factor = ntile / (per_batch * math.sqrt(points * feat * batches * nm * npts))
    vm = pl.BlockSpec(memory_space=pltpu.VMEM)
    anyw = pl.BlockSpec(memory_space=pl.ANY)
    fp = feat // npts
    dma = pltpu.SemaphoreType.DMA
    nfw = (nm - 1) * (SPLIT - 1)
    potential, centre_features = pl.pallas_call(
        functools.partial(kernel, nm, npts, factor),
        out_shape=(
            jax.ShapeDtypeStruct((slab, width), BF16),
            jax.ShapeDtypeStruct((cent, feat), BF16),
        ),
        in_specs=[anyw] * 14,
        out_specs=(vm, vm),
        scratch_shapes=[
            pltpu.SMEM((batches, per_batch), jnp.int32),
            pltpu.VMEM((batches, points), F32),
            pltpu.VMEM((batches, points), jnp.int32),
            pltpu.VMEM((1, feat), F32),
            pltpu.VMEM((1, feat), F32),
            pltpu.VMEM((feat, hid), BF16),
            pltpu.VMEM((1, hid), F32),
            pltpu.VMEM((hid, hid), BF16),
            pltpu.VMEM((1, hid), F32),
            pltpu.VMEM((feat, hid), BF16),
            pltpu.VMEM((1, feat), F32),
            [pltpu.VMEM((per_batch, points, tile), BF16) for _ in range(batches)],
            pltpu.VMEM((batches, feat, points), BF16),
            pltpu.VMEM((batches, nb, points), BF16),
            pltpu.VMEM((batches, ncent, points), BF16),
            pltpu.VMEM((batches, 1, points), F32),
            pltpu.VMEM((batches, 1, points), F32),
            pltpu.VMEM((nb, nb), BF16),
            pltpu.VMEM((feat, ncent), F32),
            pltpu.VMEM((npts, fp, ncent), F32),
            pltpu.VMEM((npts, fp, ncent), F32),
            pltpu.VMEM((fp, ncent), F32),
            pltpu.VMEM((nm, fp, ncent), F32),
            pltpu.VMEM((npts, fp, ncent), F32),
            pltpu.VMEM((ncent, feat), F32),
            pltpu.VMEM((feat, ncent), BF16),
            pltpu.VMEM((2, npts, slab, nb // 2), F32),
            pltpu.VMEM((npts, slab, nb // 2), BF16),
            pltpu.VMEM((npts, slab, nb // 2), BF16),
            pltpu.VMEM((npts // 2, 2, slab, nb // 2), F32),
            pltpu.VMEM((npts // 2, 2, slab, nb // 2), BF16),
            pltpu.VMEM((npts // 2, 2, slab, nb // 2), BF16),
            pltpu.VMEM((nm, slab, width), F32),
            pltpu.VMEM((nm, slab, width), BF16),
            pltpu.VMEM((nm, slab, width), BF16),
            dma((12,)), dma((batches, per_batch)), dma((batches,)),
            dma((nm,)), dma((nm,)),
            dma((nfw,)), dma((nfw,)),
            dma((npts,)), dma((npts,)),
            dma((nm - 1,)), dma((nm - 1,)),
            dma((npts,)), dma((npts,)),
            dma((3,)), dma((3,)),
            dma((npts // 2, 2)), dma((npts // 2, 2)),
            dma((nm,)), dma((nm,)),
        ],
        compiler_params=pltpu.CompilerParams(
            collective_id=0, has_side_effects=True, vmem_limit_bytes=60 * 1024 * 1024
        ),
    )(
        basis_values, descriptors.transpose(0, 2, 1), tile_ids, density_matrix, grid_weights, centre_ids,
        density_scale.reshape(1, -1), norm_gain.reshape(1, -1),
        w_first, b_first.reshape(1, -1), w_second, b_second.reshape(1, -1),
        w_third.T, b_third.reshape(1, -1),
    )
    potential, centre_features = pl.pallas_call(
        place,
        out_shape=(
            jax.ShapeDtypeStruct((slab, width), BF16),
            jax.ShapeDtypeStruct((cent, feat), BF16),
        ),
        in_specs=[vm, vm],
        out_specs=(vm, vm),
    )(potential, centre_features)
    return (potential.T, centre_features)


def solution(mesh):
    return jax.shard_map(
        functools.partial(shards, mesh.shape["mat"], mesh.shape["pts"]),
        mesh=mesh,
        in_specs=(
            P(("mat", "pts"), None, None),
            P(("mat", "pts"), None),
            P("mat", None),
            P(("mat", "pts"), None, None),
            P(("mat", "pts"), None),
            P(("mat", "pts"), None),
            P(), P(), P(), P(), P(), P(), P(), P(),
        ),
        out_specs=(P("mat", "pts"), P("pts", None)),
        check_vma=False,
    )
```

```python
import functools
import math

import jax
import jax.numpy as jnp
from jax import lax
from jax.experimental import pallas as pl
from jax.experimental.pallas import tpu as pltpu
from jax.sharding import PartitionSpec as P

SPLIT = 2
MESH = pl.DeviceIdType.MESH
F32 = jnp.float32
BF16 = jnp.bfloat16
NT_DIMS = (((1,), (1,)), ((), ()))


def silu(v):
    h = 0.5 * v
    return h + h * jnp.tanh(h)


def place(pot, cf, out_pot, out_cf, sem):
    copies = [pltpu.make_async_copy(pot, out_pot, sem.at[0]), pltpu.make_async_copy(cf, out_cf, sem.at[1])]
    for c in copies:
        c.start()
    for c in copies:
        c.wait()


def kernel(
    nm, npts, factor,
    v_hbm, d_hbm, tiles_hbm, dm_hbm, gw_hbm, ids_hbm, scale_hbm, gain_hbm,
    w1_hbm, b1_hbm, w2_hbm, b2_hbm, w3_hbm, b3_hbm,
    out_pot, out_cf,
    tiles, gw, ids, w13, b12, sgb, w2,
    vbuf, dbuf, vt, oh, dens, pps, panel, cpart, cs_src, cs_in, cz_src, cz_in,
    full, cf_s, cft, acc, psnd, pin, whole, snd, rin, red, zsnd, zin,
    isem, msem, vsem, ag_s, ag_r, fw_s, fw_r, cs_s, cs_r, cz_s, cz_r, cg_s, cg_r, pr_s, pr_r, rp_s, rp_r, rz_s, rz_r,
):
    m = lax.axis_index("mat")
    p = lax.axis_index("pts")
    batches = len(vbuf)
    per_batch, points, tile = vbuf[0].shape
    rows, nb = dm_hbm.shape
    ntile = nb // tile
    feat = dbuf.shape[1]
    ncent = oh.shape[1]
    slab = nb // npts
    piece = rows // SPLIT

    small = [
        pltpu.make_async_copy(a, b, isem.at[i]) for i, (a, b) in enumerate((
            (tiles_hbm, tiles), (ids_hbm, ids), (dm_hbm, panel.at[pl.ds(pl.multiple_of(m * rows, rows), rows)]),
            (gw_hbm, gw), (w2_hbm, w2), (d_hbm, dbuf)))]
    grouped = [
        pltpu.make_async_copy(a, b, msem.at[i]) for a, b, i in (
            (w1_hbm, w13.at[0], 0), (w3_hbm, w13.at[1], 0), (b1_hbm, b12.at[0], 1), (b2_hbm, b12.at[1], 1),
            (scale_hbm, sgb.at[0], 2), (gain_hbm, sgb.at[1], 2), (b3_hbm, sgb.at[2], 2))]

    def vcopy(b, j):
        return pltpu.make_async_copy(v_hbm.at[b, :, pl.ds(j * tile, tile)], vbuf[b].at[j], vsem.at[b])

    barrier = pltpu.get_barrier_semaphore()
    for k in range(1, npts):
        pl.semaphore_signal(barrier, inc=1, device_id={"pts": lax.rem(p + k, npts)}, device_id_type=MESH)
    for k in range(1, nm):
        pl.semaphore_signal(barrier, inc=1, device_id={"mat": lax.rem(m + k, nm)}, device_id_type=MESH)
    for c in small[:3]:
        c.start()
    for j in range(per_batch):
        vcopy(0, j).start()
    pl.semaphore_wait(barrier, npts + nm - 2)

    def remote(src, dst, s, r, **where):
        return pltpu.make_async_remote_copy(
            src_ref=src, dst_ref=dst, send_sem=s, recv_sem=r, device_id=where, device_id_type=MESH
        )

    def at_rows(owner, part):
        return pl.ds(pl.multiple_of(owner * rows + part * piece, piece), piece)

    g = lax.rem(p, SPLIT)
    base = p - g
    near = m + 1 - 2 * lax.rem(m, 2)
    order = [near] + [lax.rem(m + 2 * (k // 2) + lax.rem(m + k, 2) - lax.rem(m, 2) + nm, nm) for k in range(2, nm)]
    ag = []
    for k, to in enumerate(order):
        ag.append(remote(
            dm_hbm.at[pl.ds(pl.multiple_of(g * piece, piece), piece)], panel.at[at_rows(m, g)],
            ag_s, ag_r.at[m], mat=to))
    for c in ag:
        c.start()
    for b in range(1, batches):
        for j in range(per_batch):
            vcopy(b, j).start()
    for c in small[3:] + grouped:
        c.start()
    small[0].wait()

    def part(b, owner, which=slice(None)):
        at = pl.ds(pl.multiple_of(owner * rows, rows), rows)
        q = jnp.dot(panel[at, :], vt[b][:, which], preferred_element_type=F32)
        return jnp.sum(q * vt[b][at, which].astype(F32), axis=0, keepdims=True)

    def prepare(b):
        pltpu.make_async_copy(vbuf[b], vbuf[b], vsem.at[b]).wait()
        held = [tiles[b, j] for j in range(per_batch)]

        def find(t, value, otherwise):
            for j in range(per_batch):
                otherwise = jnp.where(held[j] == t, value(j), otherwise)
            return otherwise

        spot = [find(t, lambda j: j, 0) for t in range(ntile)]
        here = [find(t, lambda j: 1, 0) for t in range(ntile)]
        for t in range(ntile):
            x = vbuf[b][spot[t]]
            if ntile != per_batch:
                x = jnp.where(here[t] == 1, x, jnp.zeros_like(x))
            vt[b][t * tile:(t + 1) * tile, :] = x.T

    def mask(b):
        which = lax.broadcasted_iota(jnp.int32, (ncent, points), 0)
        oh[b] = jnp.where(which == ids[b:b + 1, :], 1.0, 0.0).astype(BF16)

    fw = []

    def ahead(k):
        src = order[k]
        return remote(
            dm_hbm.at[pl.ds(0, piece)], panel.at[at_rows(src, g)], ag_s, ag_r.at[src], mat=src)

    def receive(k):
        ahead(k).wait_recv()
        held = panel.at[at_rows(order[k], g)]
        mine = []
        for h in range(1, SPLIT):
            i = k * (SPLIT - 1) + h - 1
            c = remote(held, held, fw_s, fw_r.at[i], pts=base + lax.rem(g + h, SPLIT))
            c.start()
            mine.append(c)
        fw.extend(mine)
        return mine

    for b in range(batches):
        if b == 1:
            small[1].wait()
            small[2].wait()
        if b:
            dens[b - 1] = part(b - 1, m)
            mask(b - 1)
        prepare(b)
        if b == batches - 2:
            passing = receive(0)
    for c in small[3:]:
        c.wait()
    pltpu.make_async_copy(w13, w13, msem.at[0]).wait()
    pltpu.make_async_copy(b12, b12, msem.at[1]).wait()
    pltpu.make_async_copy(sgb, sgb, msem.at[2]).wait()
    scale, gain, b3 = sgb.at[0], sgb.at[1], sgb.at[2]
    w1, w3 = w13.at[0], w13.at[1]
    b1, b2 = b12.at[0], b12.at[1]

    scale_col = jnp.broadcast_to(scale[...], (128, feat)).T[:, :1]
    cpart[...] = jnp.zeros_like(cpart)

    dens[batches - 1] = part(batches - 1, m)
    mask(batches - 1)
    for k in range(nm - 2):
        for c in passing:
            c.wait_recv()
        passing = receive(k + 1)
        for b in range(batches):
            dens[b] += part(b, order[k])
    for c in passing:
        c.wait_recv()
    for b in range(batches):
        d = dens[b] + part(b, order[nm - 2])
        dens[b] = d
        wf = gw[pl.ds(b, 1), :] * silu(d * scale_col + dbuf[b].astype(F32))
        high = wf.astype(BF16)
        low = (wf - high.astype(F32)).astype(BF16)
        both = lax.dot_general(
            jnp.concatenate([high, low], axis=0), oh[b], NT_DIMS, preferred_element_type=F32)
        cpart[...] += both[:feat] + both[feat:]

    far = sorted(range(1, npts), key=lambda k: -min(k, npts - k))
    fp = feat // npts
    for i in range(npts):
        cs_src[i] = cpart[i * fp:(i + 1) * fp, :]
    for k in far:
        to = lax.rem(p + k, npts)
        remote(cs_src.at[to], cs_in.at[k - 1], cs_s, cs_r, pts=to).start()
    all_cs = remote(cs_in, cs_in, cs_s, cs_r, pts=lax.rem(p + 1, npts))
    all_cs.wait_recv()
    mine = cs_src[p]
    for k in range(1, npts):
        mine = mine + cs_in[k - 1]
    cz_src[...] = mine
    for k in sorted(range(1, nm), key=lambda k: -min(k, nm - k)):
        to = lax.rem(m + k, nm)
        remote(cz_src, cz_in.at[k - 1], cz_s, cz_r, mat=to).start()
    all_cz = remote(cz_in, cz_in, cz_s, cz_r, mat=lax.rem(m + 1, nm))
    all_cz.wait_recv()
    total = mine
    for k in range(1, nm):
        total = total + cz_in[k - 1]
    full[npts - 1] = total
    for k in far:
        remote(full.at[npts - 1], full.at[k - 1], cg_s, cg_r, pts=lax.rem(p + k, npts)).start()
    others = full.at[pl.ds(0, npts - 1)]
    all_cg = remote(others, others, cg_s, cg_r, pts=lax.rem(p + 1, npts))
    all_cg.wait_recv()

    summed = jnp.concatenate([full[lax.rem(p - i - 1 + npts, npts)] for i in range(npts)], axis=0).T
    inverse = lax.rsqrt(jnp.mean(summed * summed, axis=1, keepdims=True) + 1e-05)
    normed = (summed * inverse * gain[...]).astype(BF16)
    one = silu(jnp.dot(normed, w1[...], preferred_element_type=F32) + b1[...]).astype(BF16)
    two = silu(jnp.dot(one, w2[...], preferred_element_type=F32) + b2[...]).astype(BF16)
    cf = (lax.dot_general(two, w3[...], NT_DIMS, preferred_element_type=F32) + b3[...]).astype(BF16).astype(F32)
    cf_s[...] = cf
    cft[...] = cf.T.astype(BF16)
    cent = out_cf.shape[0]
    out_cf[...] = cf_s[pl.ds(pl.multiple_of(p * cent, cent), cent), :].astype(BF16)

    def spot(u, i):
        return 2 * i + (i + u) % 2 if isinstance(u, int) else 2 * i + lax.rem(i + u, 2)

    pairs = npts // 2
    mid = pairs // 2
    core = lax.rem(p, 2)
    chip = p // 2
    buddy = p + 1 - 2 * core

    for b in range(batches):
        nearest = jnp.dot(cft[...], oh[b], preferred_element_type=F32)
        along = jnp.sum(nearest * dbuf[b].astype(F32), axis=0, keepdims=True)
        pps[b] = gw[pl.ds(b, 1), :] * dens[b] * along * factor

    def side(b, u):
        return jnp.concatenate([
            vt[b][pl.ds(pl.multiple_of(spot(u, i) * tile, tile), tile), :] for i in range(mid)], axis=0)

    def quarter(u, w):
        r = 0
        for b in range(batches):
            left = (side(b, u).astype(F32) * pps[b]).astype(BF16)
            r = r + lax.dot_general(left, side(b, w), NT_DIMS, preferred_element_type=F32)
        return r

    def keep(r, first):
        for i in range(mid):
            for q in range(2):
                acc[q, first + i] = r[(2 * i + q) * slab:(2 * i + q + 1) * slab]

    stages = [
        (0, [(spot(0, i), 1) for i in range(mid)] + [(spot(1, i), 0) for i in range(mid)]),
        (2 * mid, [(spot(0, i), 0) for i in range(mid)]),
        (3 * mid, [(spot(1, i), 1) for i in range(mid)]),
    ]

    def pair(n):
        first, entries = stages[n]
        at = pl.ds(first, len(entries))
        return remote(psnd.at[at], pin.at[at], pr_s, pr_r.at[n], pts=buddy)

    def give(n):
        first, entries = stages[n]
        for e in range(first, first + len(entries)):
            psnd[e] = acc[1 - core, e].astype(BF16)
        pair(n).start()

    def plane(to, u):
        return remote(snd.at[to, u], rin.at[u, lax.rem(to - chip - 1 + pairs, pairs)], rp_s, rp_r.at[u], pts=2 * to + core)

    def spread(n):
        first, entries = stages[n]
        pair(n).wait_recv()
        for e, (to, u) in enumerate(entries):
            both = acc[core, first + e] + pin[first + e].astype(F32)
            whole[to, u] = both
            snd[to, u] = both.astype(BF16)
        for to, u in entries:
            @pl.when(to != chip)
            def _():
                plane(to, u).start()


    def turn(n, carry):
        keep(quarter(n // 2, jnp.where(n == 1, 0, 1)), jnp.where(n == 0, 0, (n + 1) * mid))

        @pl.when(n == 0)
        def _():
            across = jnp.concatenate([acc[q, i] for i in range(mid) for q in range(2)], axis=0)
            keep(across.T, mid)
            give(0)

        @pl.when(n == 1)
        def _():
            spread(0)
            give(1)

        @pl.when(n == 2)
        def _():
            give(2)
            spread(1)

        return carry

    lax.fori_loop(0, 3, turn, 0)
    spread(2)
    early = lax.rem(chip + chip // 2 + 1, 2)
    for n in range(2):
        u = early if n == 0 else 1 - early
        mine = whole[chip, u]
        remote(rin.at[u], rin.at[u], rp_s, rp_r.at[u], pts=buddy).wait_recv()
        for k in range(pairs - 1):
            mine = mine + rin[u, k].astype(F32)
        for i in range(mid):
            to = 2 * i + lax.rem(i + u, 2)
            red[to] = mine[:, i * tile:(i + 1) * tile]
            zsnd[to] = mine[:, i * tile:(i + 1) * tile].astype(BF16)

            @pl.when(to != m)
            def _():
                remote(zsnd.at[to], zin.at[lax.rem(to - m - 1 + nm, nm)], rz_s, rz_r, mat=to).start()
    mine = red[m]
    all_rz = remote(zin, zin, rz_s, rz_r, mat=lax.rem(m + 1, nm))
    all_rz.wait_recv()
    for k in range(nm - 1):
        mine = mine + zin[k].astype(F32)
    out_pot[...] = mine.astype(BF16)

    for c in (all_cs, all_cz, all_cg, all_rz):
        c.wait_send()
    sent = panel.at[pl.ds(0, (nm - 1) * piece)]
    remote(sent, sent, ag_s, ag_r.at[m], mat=lax.rem(m + 1, nm)).wait_send()
    sent = panel.at[pl.ds(0, (nm - 1) * (SPLIT - 1) * piece)]
    remote(sent, sent, fw_s, fw_r.at[0], pts=buddy).wait_send()
    remote(psnd, pin, pr_s, pr_r.at[0], pts=buddy).wait_send()
    remote(rin, rin, rp_s, rp_r.at[0], pts=buddy).wait_send()


def shards(
    nm, npts,
    basis_values, tile_ids, density_matrix, descriptors, grid_weights, centre_ids,
    density_scale, norm_gain, w_first, b_first, w_second, b_second, w_third, b_third,
):
    batches, points, orbitals = basis_values.shape
    per_batch = tile_ids.shape[1]
    tile = orbitals // per_batch
    rows, nb = density_matrix.shape
    feat = descriptors.shape[2]
    hid = w_first.shape[1]
    ntile = nb // tile
    cent = 16
    ncent = cent * npts
    slab = nb // npts
    width = nb // nm
    factor = ntile / (per_batch * math.sqrt(points * feat * batches * nm * npts))
    vm = pl.BlockSpec(memory_space=pltpu.VMEM)
    anyw = pl.BlockSpec(memory_space=pl.ANY)
    fp = feat // npts
    dma = pltpu.SemaphoreType.DMA
    nfw = (nm - 1) * (SPLIT - 1)
    potential, centre_features = pl.pallas_call(
        functools.partial(kernel, nm, npts, factor),
        out_shape=(pltpu.VMEM((slab, width), BF16), pltpu.VMEM((cent, feat), BF16)),
        in_specs=[anyw] * 14,
        out_specs=(vm, vm),
        scratch_shapes=[
            pltpu.SMEM((batches, per_batch), jnp.int32),
            pltpu.VMEM((batches, points), F32),
            pltpu.VMEM((batches, points), jnp.int32),
            pltpu.VMEM((2, feat, hid), BF16),
            pltpu.VMEM((2, 1, hid), F32),
            pltpu.VMEM((3, 1, feat), F32),
            pltpu.VMEM((hid, hid), BF16),
            [pltpu.VMEM((per_batch, points, tile), BF16) for _ in range(batches)],
            pltpu.VMEM((batches, feat, points), BF16),
            [pltpu.VMEM((nb, points), BF16) for _ in range(batches)],
            pltpu.VMEM((batches, ncent, points), BF16),
            pltpu.VMEM((batches, 1, points), F32),
            pltpu.VMEM((batches, 1, points), F32),
            pltpu.VMEM((nb, nb), BF16),
            pltpu.VMEM((feat, ncent), F32),
            pltpu.VMEM((npts, fp, ncent), F32),
            pltpu.VMEM((npts - 1, fp, ncent), F32),
            pltpu.VMEM((fp, ncent), F32),
            pltpu.VMEM((nm - 1, fp, ncent), F32),
            pltpu.VMEM((npts, fp, ncent), F32),
            pltpu.VMEM((ncent, feat), F32),
            pltpu.VMEM((feat, ncent), BF16),
            pltpu.VMEM((2, npts, slab, nb // 2), F32),
            pltpu.VMEM((npts, slab, nb // 2), BF16),
            pltpu.VMEM((npts, slab, nb // 2), BF16),
            pltpu.VMEM((npts // 2, 2, slab, nb // 2), F32),
            pltpu.VMEM((npts // 2, 2, slab, nb // 2), BF16),
            pltpu.VMEM((2, npts // 2 - 1, slab, nb // 2), BF16),
            pltpu.VMEM((nm, slab, width), F32),
            pltpu.VMEM((nm, slab, width), BF16),
            pltpu.VMEM((nm - 1, slab, width), BF16),
            dma((6,)), dma((3,)), dma((batches,)),
            dma, dma((nm,)), dma, dma((nfw,)),
            dma, dma, dma, dma, dma, dma,
            dma, dma((3,)), dma, dma((2,)), dma, dma,
        ],
        compiler_params=pltpu.CompilerParams(
            collective_id=0, has_side_effects=True, vmem_limit_bytes=60 * 1024 * 1024
        ),
    )(
        basis_values, descriptors.transpose(0, 2, 1), tile_ids, density_matrix, grid_weights, centre_ids,
        density_scale.reshape(1, -1), norm_gain.reshape(1, -1),
        w_first, b_first.reshape(1, -1), w_second, b_second.reshape(1, -1),
        w_third.T, b_third.reshape(1, -1),
    )
    potential, centre_features = pl.pallas_call(
        place,
        out_shape=(
            jax.ShapeDtypeStruct((slab, width), BF16),
            jax.ShapeDtypeStruct((cent, feat), BF16),
        ),
        in_specs=[vm, vm],
        out_specs=(anyw, anyw),
        scratch_shapes=[dma((2,))],
    )(
        pltpu.with_memory_space_constraint(potential, pltpu.VMEM),
        pltpu.with_memory_space_constraint(centre_features, pltpu.VMEM),
    )
    return (potential.T, centre_features)


def solution(mesh):
    return jax.shard_map(
        functools.partial(shards, mesh.shape["mat"], mesh.shape["pts"]),
        mesh=mesh,
        in_specs=(
            P(("mat", "pts"), None, None),
            P(("mat", "pts"), None),
            P("mat", None),
            P(("mat", "pts"), None, None),
            P(("mat", "pts"), None),
            P(("mat", "pts"), None),
            P(), P(), P(), P(), P(), P(), P(), P(),
        ),
        out_specs=(P("mat", "pts"), P("pts", None)),
        check_vma=False,
    )
```

```python
import functools
import math

import jax
import jax.numpy as jnp
from jax import lax
from jax.experimental import pallas as pl
from jax.experimental.pallas import tpu as pltpu
from jax.sharding import PartitionSpec as P

SPLIT = 2
MESH = pl.DeviceIdType.MESH
F32 = jnp.float32
BF16 = jnp.bfloat16
NT_DIMS = (((1,), (1,)), ((), ()))


def silu(v):
    h = 0.5 * v
    return h + h * jnp.tanh(h)


def place(pot, cf, out_pot, out_cf, sem):
    copies = [pltpu.make_async_copy(pot, out_pot, sem.at[0]), pltpu.make_async_copy(cf, out_cf, sem.at[1])]
    for c in copies:
        c.start()
    for c in copies:
        c.wait()


def kernel(
    nm, npts, factor,
    v_hbm, d_hbm, tiles_hbm, dm_hbm, gw_hbm, ids_hbm, scale_hbm, gain_hbm,
    w1_hbm, b1_hbm, w2_hbm, b2_hbm, w3_hbm, b3_hbm,
    out_pot, out_cf,
    tiles, gw, ids, w13, b12, sgb, w2,
    vbuf, dbuf, vt, oh, dens, pps, panel, cpart, cs_src, cs_in, cz_src, cz_in,
    full, cf_s, cft, acc, psnd, pin, whole, snd, rin, red, zsnd, zin,
    isem, msem, vsem, ag_s, ag_r, fw_s, fw_r, cs_s, cs_r, cz_s, cz_r, cg_s, cg_r, pr_s, pr_r, rp_s, rp_r, rz_s, rz_r,
):
    m = lax.axis_index("mat")
    p = lax.axis_index("pts")
    batches = len(vbuf)
    per_batch, points, tile = vbuf[0].shape
    rows, nb = dm_hbm.shape
    ntile = nb // tile
    feat = dbuf.shape[1]
    ncent = oh.shape[1]
    slab = nb // npts
    piece = rows // SPLIT

    small = [
        pltpu.make_async_copy(a, b, isem.at[i]) for i, (a, b) in enumerate((
            (tiles_hbm, tiles), (ids_hbm, ids), (dm_hbm, panel.at[pl.ds(pl.multiple_of(m * rows, rows), rows)]),
            (gw_hbm, gw), (w2_hbm, w2), (d_hbm, dbuf)))]
    grouped = [
        pltpu.make_async_copy(a, b, msem.at[i]) for a, b, i in (
            (w1_hbm, w13.at[0], 0), (w3_hbm, w13.at[1], 0), (b1_hbm, b12.at[0], 1), (b2_hbm, b12.at[1], 1),
            (scale_hbm, sgb.at[0], 2), (gain_hbm, sgb.at[1], 2), (b3_hbm, sgb.at[2], 2))]

    def vcopy(b, j):
        return pltpu.make_async_copy(v_hbm.at[b, :, pl.ds(j * tile, tile)], vbuf[b].at[j], vsem.at[b])

    barrier = pltpu.get_barrier_semaphore()
    for k in range(1, npts):
        pl.semaphore_signal(barrier, inc=1, device_id={"pts": lax.rem(p + k, npts)}, device_id_type=MESH)
    for k in range(1, nm):
        pl.semaphore_signal(barrier, inc=1, device_id={"mat": lax.rem(m + k, nm)}, device_id_type=MESH)
    for c in small[:3]:
        c.start()
    for j in range(per_batch):
        vcopy(0, j).start()
    pl.semaphore_wait(barrier, npts + nm - 2)

    def remote(src, dst, s, r, **where):
        return pltpu.make_async_remote_copy(
            src_ref=src, dst_ref=dst, send_sem=s, recv_sem=r, device_id=where, device_id_type=MESH
        )

    def at_rows(owner, part):
        return pl.ds(pl.multiple_of(owner * rows + part * piece, piece), piece)

    g = lax.rem(p, SPLIT)
    base = p - g
    near = m + 1 - 2 * lax.rem(m, 2)
    order = [near] + [lax.rem(m + 2 * (k // 2) + lax.rem(m + k, 2) - lax.rem(m, 2) + nm, nm) for k in range(2, nm)]
    ag = []
    for k, to in enumerate(order):
        ag.append(remote(
            dm_hbm.at[pl.ds(pl.multiple_of(g * piece, piece), piece)], panel.at[at_rows(m, g)],
            ag_s, ag_r.at[m], mat=to))
    for c in ag:
        c.start()
    for b in range(1, batches):
        for j in range(per_batch):
            vcopy(b, j).start()
    for c in small[3:] + grouped:
        c.start()
    small[0].wait()

    def part(b, owner, which=slice(None)):
        at = pl.ds(pl.multiple_of(owner * rows, rows), rows)
        q = jnp.dot(panel[at, :], vt[b][:, which], preferred_element_type=F32)
        return jnp.sum(q * vt[b][at, which].astype(F32), axis=0, keepdims=True)

    def prepare(b):
        held = [tiles[b, j] for j in range(per_batch)]

        def find(t, value, otherwise):
            for j in range(per_batch):
                otherwise = jnp.where(held[j] == t, value(j), otherwise)
            return otherwise

        spot = [find(t, lambda j: j, 0) for t in range(ntile)]
        here = [find(t, lambda j: 1, 0) for t in range(ntile)]
        for t in range(ntile):
            x = vbuf[b][spot[t]]
            if ntile != per_batch:
                x = jnp.where(here[t] == 1, x, jnp.zeros_like(x))
            vt[b][t * tile:(t + 1) * tile, :] = x.T

    def mask(b):
        which = lax.broadcasted_iota(jnp.int32, (ncent, points), 0)
        oh[b] = jnp.where(which == ids[b:b + 1, :], 1.0, 0.0).astype(BF16)

    fw = []

    def ahead(k):
        src = order[k]
        return remote(
            dm_hbm.at[pl.ds(0, piece)], panel.at[at_rows(src, g)], ag_s, ag_r.at[src], mat=src)

    def receive(k):
        ahead(k).wait_recv()
        held = panel.at[at_rows(order[k], g)]
        mine = []
        for h in range(1, SPLIT):
            i = k * (SPLIT - 1) + h - 1
            c = remote(held, held, fw_s, fw_r.at[i], pts=base + lax.rem(g + h, SPLIT))
            c.start()
            mine.append(c)
        fw.extend(mine)
        return mine

    for b in range(batches):
        if b == 1:
            small[1].wait()
            small[2].wait()
        pltpu.make_async_copy(vbuf[b], vbuf[b], vsem.at[b]).wait()
        if b:
            dens[b - 1] = part(b - 1, m)
            mask(b - 1)
        prepare(b)
    passing = receive(0)
    for c in small[3:]:
        c.wait()
    pltpu.make_async_copy(w13, w13, msem.at[0]).wait()
    pltpu.make_async_copy(b12, b12, msem.at[1]).wait()
    pltpu.make_async_copy(sgb, sgb, msem.at[2]).wait()
    scale, gain, b3 = sgb.at[0], sgb.at[1], sgb.at[2]
    w1, w3 = w13.at[0], w13.at[1]
    b1, b2 = b12.at[0], b12.at[1]

    scale_col = jnp.broadcast_to(scale[...], (128, feat)).T[:, :1]
    cpart[...] = jnp.zeros_like(cpart)

    dens[batches - 1] = part(batches - 1, m)
    mask(batches - 1)
    for k in range(nm - 2):
        for c in passing:
            c.wait_recv()
        passing = receive(k + 1)
        for b in range(batches):
            dens[b] += part(b, order[k])
    for c in passing:
        c.wait_recv()
    for b in range(batches):
        d = dens[b] + part(b, order[nm - 2])
        dens[b] = d
        wf = gw[pl.ds(b, 1), :] * silu(d * scale_col + dbuf[b].astype(F32))
        high = wf.astype(BF16)
        low = (wf - high.astype(F32)).astype(BF16)
        both = lax.dot_general(
            jnp.concatenate([high, low], axis=0), oh[b], NT_DIMS, preferred_element_type=F32)
        cpart[...] += both[:feat] + both[feat:]

    far = sorted(range(1, npts), key=lambda k: -min(k, npts - k))
    fp = feat // npts
    for i in range(npts):
        cs_src[i] = cpart[i * fp:(i + 1) * fp, :]
    for k in far:
        to = lax.rem(p + k, npts)
        remote(cs_src.at[to], cs_in.at[k - 1], cs_s, cs_r, pts=to).start()
    all_cs = remote(cs_in, cs_in, cs_s, cs_r, pts=lax.rem(p + 1, npts))
    all_cs.wait_recv()
    mine = cs_src[p]
    for k in range(1, npts):
        mine = mine + cs_in[k - 1]
    cz_src[...] = mine
    for k in sorted(range(1, nm), key=lambda k: -min(k, nm - k)):
        to = lax.rem(m + k, nm)
        remote(cz_src, cz_in.at[k - 1], cz_s, cz_r, mat=to).start()
    all_cz = remote(cz_in, cz_in, cz_s, cz_r, mat=lax.rem(m + 1, nm))
    all_cz.wait_recv()
    total = mine
    for k in range(1, nm):
        total = total + cz_in[k - 1]
    full[npts - 1] = total
    for k in far:
        remote(full.at[npts - 1], full.at[k - 1], cg_s, cg_r, pts=lax.rem(p + k, npts)).start()
    others = full.at[pl.ds(0, npts - 1)]
    all_cg = remote(others, others, cg_s, cg_r, pts=lax.rem(p + 1, npts))
    all_cg.wait_recv()

    summed = jnp.concatenate([full[lax.rem(p - i - 1 + npts, npts)] for i in range(npts)], axis=0).T
    inverse = lax.rsqrt(jnp.mean(summed * summed, axis=1, keepdims=True) + 1e-05)
    normed = (summed * inverse * gain[...]).astype(BF16)
    one = silu(jnp.dot(normed, w1[...], preferred_element_type=F32) + b1[...]).astype(BF16)
    two = silu(jnp.dot(one, w2[...], preferred_element_type=F32) + b2[...]).astype(BF16)
    cf = (lax.dot_general(two, w3[...], NT_DIMS, preferred_element_type=F32) + b3[...]).astype(BF16).astype(F32)
    cf_s[...] = cf
    cft[...] = cf.T.astype(BF16)
    cent = out_cf.shape[0]
    out_cf[...] = cf_s[pl.ds(pl.multiple_of(p * cent, cent), cent), :].astype(BF16)

    def spot(u, i):
        return 2 * i + (i + u) % 2 if isinstance(u, int) else 2 * i + lax.rem(i + u, 2)

    pairs = npts // 2
    mid = pairs // 2
    core = lax.rem(p, 2)
    chip = p // 2
    buddy = p + 1 - 2 * core

    for b in range(batches):
        nearest = jnp.dot(cft[...], oh[b], preferred_element_type=F32)
        along = jnp.sum(nearest * dbuf[b].astype(F32), axis=0, keepdims=True)
        pps[b] = gw[pl.ds(b, 1), :] * dens[b] * along * factor

    def side(b, u):
        return jnp.concatenate([
            vt[b][pl.ds(pl.multiple_of(spot(u, i) * tile, tile), tile), :] for i in range(mid)], axis=0)

    def quarter(u, w):
        r = 0
        for b in range(batches):
            left = (side(b, u).astype(F32) * pps[b]).astype(BF16)
            r = r + lax.dot_general(left, side(b, w), NT_DIMS, preferred_element_type=F32)
        return r

    def keep(r, first):
        for i in range(mid):
            for q in range(2):
                acc[q, first + i] = r[(2 * i + q) * slab:(2 * i + q + 1) * slab]

    stages = [
        (0, [(spot(0, i), 0) for i in range(mid)]),
        (mid, [(spot(1, i), 0) for i in range(mid)] + [(spot(0, i), 1) for i in range(mid)]),
        (3 * mid, [(spot(1, i), 1) for i in range(mid)]),
    ]

    def pair(n):
        first, entries = stages[n]
        at = pl.ds(first, len(entries))
        return remote(psnd.at[at], pin.at[at], pr_s, pr_r.at[n], pts=buddy)

    def give(n):
        first, entries = stages[n]
        for e in range(first, first + len(entries)):
            psnd[e] = acc[1 - core, e].astype(BF16)
        pair(n).start()

    def plane(to, u):
        return remote(snd.at[to, u], rin.at[u, lax.rem(to - chip - 1 + pairs, pairs)], rp_s, rp_r.at[u], pts=2 * to + core)

    def spread(n):
        first, entries = stages[n]
        pair(n).wait_recv()
        for e, (to, u) in enumerate(entries):
            both = acc[core, first + e] + pin[first + e].astype(F32)
            whole[to, u] = both
            snd[to, u] = both.astype(BF16)
        for to, u in entries:
            @pl.when(to != chip)
            def _():
                plane(to, u).start()


    def turn(n, carry):
        keep(quarter(n // 2, (n + 1) // 2), jnp.where(n == 0, 0, (n + 1) * mid))

        @pl.when(n == 0)
        def _():
            give(0)

        @pl.when(n == 1)
        def _():
            across = jnp.concatenate([acc[q, 2 * mid + i] for i in range(mid) for q in range(2)], axis=0)
            keep(across.T, mid)
            give(1)
            spread(0)

        @pl.when(n == 2)
        def _():
            give(2)
            spread(1)

        return carry

    lax.fori_loop(0, 3, turn, 0)
    spread(2)
    for u in range(2):
        mine = whole[chip, u]
        remote(rin.at[u], rin.at[u], rp_s, rp_r.at[u], pts=buddy).wait_recv()
        for k in range(pairs - 1):
            mine = mine + rin[u, k].astype(F32)
        for i in range(mid):
            to = 2 * i + lax.rem(i + u, 2)
            red[to] = mine[:, i * tile:(i + 1) * tile]
            zsnd[to] = mine[:, i * tile:(i + 1) * tile].astype(BF16)

            @pl.when(to != m)
            def _():
                remote(zsnd.at[to], zin.at[lax.rem(to - m - 1 + nm, nm)], rz_s, rz_r, mat=to).start()
    mine = red[m]
    all_rz = remote(zin, zin, rz_s, rz_r, mat=lax.rem(m + 1, nm))
    all_rz.wait_recv()
    for k in range(nm - 1):
        mine = mine + zin[k].astype(F32)
    out_pot[...] = mine.astype(BF16)

    for c in (all_cs, all_cz, all_cg, all_rz):
        c.wait_send()
    sent = panel.at[pl.ds(0, (nm - 1) * piece)]
    remote(sent, sent, ag_s, ag_r.at[m], mat=lax.rem(m + 1, nm)).wait_send()
    sent = panel.at[pl.ds(0, (nm - 1) * (SPLIT - 1) * piece)]
    remote(sent, sent, fw_s, fw_r.at[0], pts=buddy).wait_send()
    remote(psnd, pin, pr_s, pr_r.at[0], pts=buddy).wait_send()
    remote(rin, rin, rp_s, rp_r.at[0], pts=buddy).wait_send()


def shards(
    nm, npts,
    basis_values, tile_ids, density_matrix, descriptors, grid_weights, centre_ids,
    density_scale, norm_gain, w_first, b_first, w_second, b_second, w_third, b_third,
):
    batches, points, orbitals = basis_values.shape
    per_batch = tile_ids.shape[1]
    tile = orbitals // per_batch
    rows, nb = density_matrix.shape
    feat = descriptors.shape[2]
    hid = w_first.shape[1]
    ntile = nb // tile
    cent = 16
    ncent = cent * npts
    slab = nb // npts
    width = nb // nm
    factor = ntile / (per_batch * math.sqrt(points * feat * batches * nm * npts))
    vm = pl.BlockSpec(memory_space=pltpu.VMEM)
    anyw = pl.BlockSpec(memory_space=pl.ANY)
    fp = feat // npts
    dma = pltpu.SemaphoreType.DMA
    nfw = (nm - 1) * (SPLIT - 1)
    potential, centre_features = pl.pallas_call(
        functools.partial(kernel, nm, npts, factor),
        out_shape=(pltpu.VMEM((slab, width), BF16), pltpu.VMEM((cent, feat), BF16)),
        in_specs=[anyw] * 14,
        out_specs=(vm, vm),
        scratch_shapes=[
            pltpu.SMEM((batches, per_batch), jnp.int32),
            pltpu.VMEM((batches, points), F32),
            pltpu.VMEM((batches, points), jnp.int32),
            pltpu.VMEM((2, feat, hid), BF16),
            pltpu.VMEM((2, 1, hid), F32),
            pltpu.VMEM((3, 1, feat), F32),
            pltpu.VMEM((hid, hid), BF16),
            [pltpu.VMEM((per_batch, points, tile), BF16) for _ in range(batches)],
            pltpu.VMEM((batches, feat, points), BF16),
            [pltpu.VMEM((nb, points), BF16) for _ in range(batches)],
            pltpu.VMEM((batches, ncent, points), BF16),
            pltpu.VMEM((batches, 1, points), F32),
            pltpu.VMEM((batches, 1, points), F32),
            pltpu.VMEM((nb, nb), BF16),
            pltpu.VMEM((feat, ncent), F32),
            pltpu.VMEM((npts, fp, ncent), F32),
            pltpu.VMEM((npts - 1, fp, ncent), F32),
            pltpu.VMEM((fp, ncent), F32),
            pltpu.VMEM((nm - 1, fp, ncent), F32),
            pltpu.VMEM((npts, fp, ncent), F32),
            pltpu.VMEM((ncent, feat), F32),
            pltpu.VMEM((feat, ncent), BF16),
            pltpu.VMEM((2, npts, slab, nb // 2), F32),
            pltpu.VMEM((npts, slab, nb // 2), BF16),
            pltpu.VMEM((npts, slab, nb // 2), BF16),
            pltpu.VMEM((npts // 2, 2, slab, nb // 2), F32),
            pltpu.VMEM((npts // 2, 2, slab, nb // 2), BF16),
            pltpu.VMEM((2, npts // 2 - 1, slab, nb // 2), BF16),
            pltpu.VMEM((nm, slab, width), F32),
            pltpu.VMEM((nm, slab, width), BF16),
            pltpu.VMEM((nm - 1, slab, width), BF16),
            dma((6,)), dma((3,)), dma((batches,)),
            dma, dma((nm,)), dma, dma((nfw,)),
            dma, dma, dma, dma, dma, dma,
            dma, dma((3,)), dma, dma((2,)), dma, dma,
        ],
        compiler_params=pltpu.CompilerParams(
            collective_id=0, has_side_effects=True, vmem_limit_bytes=60 * 1024 * 1024
        ),
    )(
        basis_values, descriptors.transpose(0, 2, 1), tile_ids, density_matrix, grid_weights, centre_ids,
        density_scale.reshape(1, -1), norm_gain.reshape(1, -1),
        w_first, b_first.reshape(1, -1), w_second, b_second.reshape(1, -1),
        w_third.T, b_third.reshape(1, -1),
    )
    potential, centre_features = pl.pallas_call(
        place,
        out_shape=(
            jax.ShapeDtypeStruct((slab, width), BF16),
            jax.ShapeDtypeStruct((cent, feat), BF16),
        ),
        in_specs=[vm, vm],
        out_specs=(anyw, anyw),
        scratch_shapes=[dma((2,))],
    )(
        pltpu.with_memory_space_constraint(potential, pltpu.VMEM),
        pltpu.with_memory_space_constraint(centre_features, pltpu.VMEM),
    )
    return (potential.T, centre_features)


def solution(mesh):
    return jax.shard_map(
        functools.partial(shards, mesh.shape["mat"], mesh.shape["pts"]),
        mesh=mesh,
        in_specs=(
            P(("mat", "pts"), None, None),
            P(("mat", "pts"), None),
            P("mat", None),
            P(("mat", "pts"), None, None),
            P(("mat", "pts"), None),
            P(("mat", "pts"), None),
            P(), P(), P(), P(), P(), P(), P(), P(),
        ),
        out_specs=(P("mat", "pts"), P("pts", None)),
        check_vma=False,
    )
```

```python
import functools
import math

import jax
import jax.numpy as jnp
from jax import lax
from jax.experimental import pallas as pl
from jax.experimental.pallas import tpu as pltpu
from jax.sharding import PartitionSpec as P

SPLIT = 2
MESH = pl.DeviceIdType.MESH
F32 = jnp.float32
BF16 = jnp.bfloat16
NT_DIMS = (((1,), (1,)), ((), ()))


def silu(v):
    h = 0.5 * v
    return h + h * jnp.tanh(h)


def place(pot, cf, out_pot, out_cf, sem):
    copies = [pltpu.make_async_copy(pot, out_pot, sem.at[0]), pltpu.make_async_copy(cf, out_cf, sem.at[1])]
    for c in copies:
        c.start()
    for c in copies:
        c.wait()


def kernel(
    nm, npts, factor,
    v_hbm, d_hbm, tiles_hbm, dm_hbm, gw_hbm, ids_hbm, scale_hbm, gain_hbm,
    w1_hbm, b1_hbm, w2_hbm, b2_hbm, w3_hbm, b3_hbm,
    out_pot, out_cf,
    tiles, gw, ids, w13, b12, sgb, w2, gain_col, b3_col,
    vbuf, dbuf, vt, oh, dens, pps, panel, cpart, cs_src, cs_in, cz_src, cz_in,
    full, cf_s, cft, acc, psnd, pin, whole, snd, rin, red, zsnd, zin,
    isem, msem, vsem, ag_s, ag_r, fw_s, fw_r, cs_s, cs_r, cz_s, cz_r, cg_s, cg_r, pr_s, pr_r, rp_s, rp_r, rz_s, rz_r,
):
    m = lax.axis_index("mat")
    p = lax.axis_index("pts")
    batches = len(vbuf)
    per_batch, points, tile = vbuf[0].shape
    rows, nb = dm_hbm.shape
    ntile = nb // tile
    feat = dbuf.shape[1]
    ncent = oh.shape[1]
    slab = nb // npts
    piece = rows // SPLIT

    small = [
        pltpu.make_async_copy(a, b, isem.at[i]) for i, (a, b) in enumerate((
            (tiles_hbm, tiles), (ids_hbm, ids), (dm_hbm, panel.at[pl.ds(pl.multiple_of(m * rows, rows), rows)]),
            (gw_hbm, gw), (w2_hbm, w2), (d_hbm, dbuf)))]
    grouped = [
        pltpu.make_async_copy(a, b, msem.at[i]) for a, b, i in (
            (w1_hbm, w13.at[0], 0), (w3_hbm, w13.at[1], 0), (b1_hbm, b12.at[0], 1), (b2_hbm, b12.at[1], 1),
            (scale_hbm, sgb.at[0], 2), (gain_hbm, sgb.at[1], 2), (b3_hbm, sgb.at[2], 2))]

    def vcopy(b, j):
        return pltpu.make_async_copy(v_hbm.at[b, :, pl.ds(j * tile, tile)], vbuf[b].at[j], vsem.at[b])

    barrier = pltpu.get_barrier_semaphore()
    for k in range(1, nm):
        pl.semaphore_signal(barrier, inc=1, device_id={"mat": lax.rem(m + k, nm)}, device_id_type=MESH)
    for k in range(1, npts):
        pl.semaphore_signal(barrier, inc=1, device_id={"pts": lax.rem(p + k, npts)}, device_id_type=MESH)
    for c in small[:3]:
        c.start()
    for j in range(per_batch):
        vcopy(0, j).start()
    pl.semaphore_wait(barrier, npts + nm - 2)

    def remote(src, dst, s, r, **where):
        return pltpu.make_async_remote_copy(
            src_ref=src, dst_ref=dst, send_sem=s, recv_sem=r, device_id=where, device_id_type=MESH
        )

    def at_rows(owner, part):
        return pl.ds(pl.multiple_of(owner * rows + part * piece, piece), piece)

    g = lax.rem(p, SPLIT)
    base = p - g
    near = m + 1 - 2 * lax.rem(m, 2)
    order = [near] + [lax.rem(m + 2 * (k // 2) + lax.rem(m + k, 2) - lax.rem(m, 2) + nm, nm) for k in range(2, nm)]
    ag = []
    for k, to in enumerate(order):
        ag.append(remote(
            dm_hbm.at[pl.ds(pl.multiple_of(g * piece, piece), piece)], panel.at[at_rows(m, g)],
            ag_s, ag_r.at[m], mat=to))
    for c in ag:
        c.start()
    for b in range(1, batches):
        for j in range(per_batch):
            vcopy(b, j).start()
    for c in small[3:] + grouped:
        c.start()
    small[0].wait()

    def part(b, owner, which=slice(None)):
        at = pl.ds(pl.multiple_of(owner * rows, rows), rows)
        q = jnp.dot(panel[at, :], vt.at[b][:, which], preferred_element_type=F32)
        return jnp.sum(q * vt.at[b][at, which].astype(F32), axis=0, keepdims=True)

    def prepare(b):
        held = [tiles[b, j] for j in range(per_batch)]

        def find(t, value, otherwise):
            for j in range(per_batch):
                otherwise = jnp.where(held[j] == t, value(j), otherwise)
            return otherwise

        spot = [find(t, lambda j: j, 0) for t in range(ntile)]
        here = [find(t, lambda j: 1, 0) for t in range(ntile)]
        for t in range(ntile):
            x = vbuf[b][spot[t]]
            if ntile != per_batch:
                x = jnp.where(here[t] == 1, x, jnp.zeros_like(x))
            vt.at[b][t * tile:(t + 1) * tile, :] = x.T

    def mask(b):
        which = lax.broadcasted_iota(jnp.int32, (ncent, points), 0)
        oh[b] = jnp.where(which == ids[b:b + 1, :], 1.0, 0.0).astype(BF16)

    fw = []

    def ahead(k):
        src = order[k]
        return remote(
            dm_hbm.at[pl.ds(0, piece)], panel.at[at_rows(src, g)], ag_s, ag_r.at[src], mat=src)

    def receive(k):
        ahead(k).wait_recv()
        held = panel.at[at_rows(order[k], g)]
        mine = []
        for h in range(1, SPLIT):
            i = k * (SPLIT - 1) + h - 1
            c = remote(held, held, fw_s, fw_r.at[i], pts=base + lax.rem(g + h, SPLIT))
            c.start()
            mine.append(c)
        fw.extend(mine)
        return mine

    for b in range(batches):
        if b == 1:
            small[1].wait()
            small[2].wait()
        pltpu.make_async_copy(vbuf[b], vbuf[b], vsem.at[b]).wait()
        if b:
            dens[b - 1] = part(b - 1, m)
            mask(b - 1)
        prepare(b)
    passing = receive(0)
    for c in small[3:]:
        c.wait()
    pltpu.make_async_copy(w13, w13, msem.at[0]).wait()
    pltpu.make_async_copy(b12, b12, msem.at[1]).wait()
    pltpu.make_async_copy(sgb, sgb, msem.at[2]).wait()
    scale, gain, b3 = sgb.at[0], sgb.at[1], sgb.at[2]
    w1, w3 = w13.at[0], w13.at[1]
    b1, b2 = b12.at[0], b12.at[1]

    def column(row):
        return jnp.broadcast_to(row[...], (128, feat)).T[:, :1]

    scale_col = column(scale)
    gain_col[...] = jnp.broadcast_to(column(gain), gain_col.shape)
    b3_col[...] = jnp.broadcast_to(column(b3), b3_col.shape)
    cpart[...] = jnp.zeros_like(cpart)

    dens[batches - 1] = part(batches - 1, m)
    mask(batches - 1)
    for k in range(nm - 2):
        for c in passing:
            c.wait_recv()
        passing = receive(k + 1)

        def step(i, carry):
            for b in (2 * i, 2 * i + 1):
                dens[b] += part(b, order[k])
            return carry

        lax.fori_loop(0, batches // 2, step, 0)
    for c in passing:
        c.wait_recv()
    for b in range(batches):
        d = dens[b] + part(b, order[nm - 2])
        dens[b] = d
        wf = gw[pl.ds(b, 1), :] * silu(d * scale_col + dbuf[b].astype(F32))
        high = wf.astype(BF16)
        low = (wf - high.astype(F32)).astype(BF16)
        both = lax.dot_general(
            jnp.concatenate([high, low], axis=0), oh[b], NT_DIMS, preferred_element_type=F32)
        cpart[...] += both[:feat] + both[feat:]

    far = sorted(range(1, npts), key=lambda k: -min(k, npts - k))
    fp = feat // npts
    for i in range(npts):
        cs_src[i] = cpart[i * fp:(i + 1) * fp, :]
    for k in far:
        to = lax.rem(p + k, npts)
        remote(cs_src.at[to], cs_in.at[k - 1], cs_s, cs_r, pts=to).start()
    all_cs = remote(cs_in, cs_in, cs_s, cs_r, pts=lax.rem(p + 1, npts))
    all_cs.wait_recv()
    mine = cs_src[p]
    for k in range(1, npts):
        mine = mine + cs_in[k - 1]
    cz_src[...] = mine
    for k in sorted(range(1, nm), key=lambda k: -min(k, nm - k)):
        to = lax.rem(m + k, nm)
        remote(cz_src, cz_in.at[k - 1], cz_s, cz_r, mat=to).start()
    all_cz = remote(cz_in, cz_in, cz_s, cz_r, mat=lax.rem(m + 1, nm))
    all_cz.wait_recv()
    total = mine
    for k in range(1, nm):
        total = total + cz_in[k - 1]
    full[npts - 1] = total
    for k in far:
        remote(full.at[npts - 1], full.at[k - 1], cg_s, cg_r, pts=lax.rem(p + k, npts)).start()
    others = full.at[pl.ds(0, npts - 1)]
    all_cg = remote(others, others, cg_s, cg_r, pts=lax.rem(p + 1, npts))
    all_cg.wait_recv()

    summed = jnp.concatenate([full[lax.rem(p - i - 1 + npts, npts)] for i in range(npts)], axis=0)
    inverse = lax.rsqrt(jnp.mean(summed * summed, axis=0, keepdims=True) + 1e-05)
    normed = (summed * inverse * gain_col[...]).T.astype(BF16)
    one = silu(jnp.dot(normed, w1[...], preferred_element_type=F32) + b1[...]).astype(BF16)
    two = silu(jnp.dot(one, w2[...], preferred_element_type=F32) + b2[...]).astype(BF16)
    cft[...] = (lax.dot_general(w3[...], two, NT_DIMS, preferred_element_type=F32) + b3_col[...]).astype(BF16)

    def spot(u, i):
        return 2 * i + (i + u) % 2 if isinstance(u, int) else 2 * i + lax.rem(i + u, 2)

    pairs = npts // 2
    mid = pairs // 2
    core = lax.rem(p, 2)
    chip = p // 2
    buddy = p + 1 - 2 * core

    for b in range(batches):
        nearest = jnp.dot(cft[...], oh[b], preferred_element_type=F32)
        along = jnp.sum(nearest * dbuf[b].astype(F32), axis=0, keepdims=True)
        pps[b] = gw[pl.ds(b, 1), :] * dens[b] * along * factor

    def side(b, u):
        return jnp.concatenate([
            vt.at[b][pl.ds(pl.multiple_of(spot(u, i) * tile, tile), tile), :] for i in range(mid)], axis=0)

    def quarter(u, w):
        r = 0
        for b in range(batches):
            left = (side(b, u).astype(F32) * pps[b]).astype(BF16)
            r = r + lax.dot_general(left, side(b, w), NT_DIMS, preferred_element_type=F32)
        return r

    def keep(r, first):
        for i in range(mid):
            for q in range(2):
                acc[q, first + i] = r[(2 * i + q) * slab:(2 * i + q + 1) * slab]

    stages = [
        (0, [(spot(0, i), 0) for i in range(mid)]),
        (mid, [(spot(1, i), 0) for i in range(mid)] + [(spot(0, i), 1) for i in range(mid)]),
        (3 * mid, [(spot(1, i), 1) for i in range(mid)]),
    ]

    def pair(n):
        first, entries = stages[n]
        at = pl.ds(first, len(entries))
        return remote(psnd.at[at], pin.at[at], pr_s, pr_r.at[n], pts=buddy)

    def give(n):
        first, entries = stages[n]
        for e in range(first, first + len(entries)):
            psnd[e] = acc[1 - core, e].astype(BF16)
        pair(n).start()

    def plane(to, u):
        return remote(snd.at[to, u], rin.at[u, lax.rem(to - chip - 1 + pairs, pairs)], rp_s, rp_r.at[u], pts=2 * to + core)

    def spread(n):
        first, entries = stages[n]
        pair(n).wait_recv()
        for e, (to, u) in enumerate(entries):
            both = acc[core, first + e] + pin[first + e].astype(F32)
            whole[to, u] = both
            snd[to, u] = both.astype(BF16)
        for to, u in entries:
            @pl.when(to != chip)
            def _():
                plane(to, u).start()


    def turn(n, carry):
        keep(quarter(n // 2, (n + 1) // 2), jnp.where(n == 0, 0, (n + 1) * mid))

        @pl.when(n == 0)
        def _():
            give(0)

        @pl.when(n == 1)
        def _():
            across = jnp.concatenate([acc[q, 2 * mid + i] for i in range(mid) for q in range(2)], axis=0)
            keep(across.T, mid)
            give(1)
            spread(0)

        @pl.when(n == 2)
        def _():
            give(2)
            spread(1)

        return carry

    lax.fori_loop(0, 3, turn, 0)
    cf_s[...] = cft[...].astype(F32).T
    cent = out_cf.shape[0]
    out_cf[...] = cf_s[pl.ds(pl.multiple_of(p * cent, cent), cent), :].astype(BF16)
    spread(2)
    for u in range(2):
        mine = whole[chip, u]
        remote(rin.at[u], rin.at[u], rp_s, rp_r.at[u], pts=buddy).wait_recv()
        for k in range(pairs - 1):
            mine = mine + rin[u, k].astype(F32)
        for i in range(mid):
            to = 2 * i + lax.rem(i + u, 2)
            red[to] = mine[:, i * tile:(i + 1) * tile]
            zsnd[to] = mine[:, i * tile:(i + 1) * tile].astype(BF16)

            @pl.when(to != m)
            def _():
                remote(zsnd.at[to], zin.at[lax.rem(to - m - 1 + nm, nm)], rz_s, rz_r, mat=to).start()
    mine = red[m]
    all_rz = remote(zin, zin, rz_s, rz_r, mat=lax.rem(m + 1, nm))
    all_rz.wait_recv()
    for k in range(nm - 1):
        mine = mine + zin[k].astype(F32)
    out_pot[...] = mine.astype(BF16)

    for c in (all_cs, all_cz, all_cg, all_rz):
        c.wait_send()
    sent = panel.at[pl.ds(0, (nm - 1) * piece)]
    remote(sent, sent, ag_s, ag_r.at[m], mat=lax.rem(m + 1, nm)).wait_send()
    sent = panel.at[pl.ds(0, (nm - 1) * (SPLIT - 1) * piece)]
    remote(sent, sent, fw_s, fw_r.at[0], pts=buddy).wait_send()
    remote(psnd, pin, pr_s, pr_r.at[0], pts=buddy).wait_send()
    remote(rin, rin, rp_s, rp_r.at[0], pts=buddy).wait_send()


def shards(
    nm, npts,
    basis_values, tile_ids, density_matrix, descriptors, grid_weights, centre_ids,
    density_scale, norm_gain, w_first, b_first, w_second, b_second, w_third, b_third,
):
    batches, points, orbitals = basis_values.shape
    per_batch = tile_ids.shape[1]
    tile = orbitals // per_batch
    rows, nb = density_matrix.shape
    feat = descriptors.shape[2]
    hid = w_first.shape[1]
    ntile = nb // tile
    cent = 16
    ncent = cent * npts
    slab = nb // npts
    width = nb // nm
    factor = ntile / (per_batch * math.sqrt(points * feat * batches * nm * npts))
    vm = pl.BlockSpec(memory_space=pltpu.VMEM)
    anyw = pl.BlockSpec(memory_space=pl.ANY)
    fp = feat // npts
    dma = pltpu.SemaphoreType.DMA
    nfw = (nm - 1) * (SPLIT - 1)
    potential, centre_features = pl.pallas_call(
        functools.partial(kernel, nm, npts, factor),
        out_shape=(pltpu.VMEM((slab, width), BF16), pltpu.VMEM((cent, feat), BF16)),
        in_specs=[anyw] * 14,
        out_specs=(vm, vm),
        scratch_shapes=[
            pltpu.SMEM((batches, per_batch), jnp.int32),
            pltpu.VMEM((batches, points), F32),
            pltpu.VMEM((batches, points), jnp.int32),
            pltpu.VMEM((2, feat, hid), BF16),
            pltpu.VMEM((2, 1, hid), F32),
            pltpu.VMEM((3, 1, feat), F32),
            pltpu.VMEM((hid, hid), BF16),
            pltpu.VMEM((feat, ncent), F32),
            pltpu.VMEM((feat, ncent), F32),
            [pltpu.VMEM((per_batch, points, tile), BF16) for _ in range(batches)],
            pltpu.VMEM((batches, feat, points), BF16),
            pltpu.VMEM((batches, nb, points), BF16),
            pltpu.VMEM((batches, ncent, points), BF16),
            pltpu.VMEM((batches, 1, points), F32),
            pltpu.VMEM((batches, 1, points), F32),
            pltpu.VMEM((nb, nb), BF16),
            pltpu.VMEM((feat, ncent), F32),
            pltpu.VMEM((npts, fp, ncent), F32),
            pltpu.VMEM((npts - 1, fp, ncent), F32),
            pltpu.VMEM((fp, ncent), F32),
            pltpu.VMEM((nm - 1, fp, ncent), F32),
            pltpu.VMEM((npts, fp, ncent), F32),
            pltpu.VMEM((ncent, feat), F32),
            pltpu.VMEM((feat, ncent), BF16),
            pltpu.VMEM((2, npts, slab, nb // 2), F32),
            pltpu.VMEM((npts, slab, nb // 2), BF16),
            pltpu.VMEM((npts, slab, nb // 2), BF16),
            pltpu.VMEM((npts // 2, 2, slab, nb // 2), F32),
            pltpu.VMEM((npts // 2, 2, slab, nb // 2), BF16),
            pltpu.VMEM((2, npts // 2 - 1, slab, nb // 2), BF16),
            pltpu.VMEM((nm, slab, width), F32),
            pltpu.VMEM((nm, slab, width), BF16),
            pltpu.VMEM((nm - 1, slab, width), BF16),
            dma((6,)), dma((3,)), dma((batches,)),
            dma, dma((nm,)), dma, dma((nfw,)),
            dma, dma, dma, dma, dma, dma,
            dma, dma((3,)), dma, dma((2,)), dma, dma,
        ],
        compiler_params=pltpu.CompilerParams(
            collective_id=0, has_side_effects=True, vmem_limit_bytes=60 * 1024 * 1024
        ),
    )(
        basis_values, descriptors.transpose(0, 2, 1), tile_ids, density_matrix, grid_weights, centre_ids,
        density_scale.reshape(1, -1), norm_gain.reshape(1, -1),
        w_first, b_first.reshape(1, -1), w_second, b_second.reshape(1, -1),
        w_third.T, b_third.reshape(1, -1),
    )
    potential, centre_features = pl.pallas_call(
        place,
        out_shape=(
            jax.ShapeDtypeStruct((slab, width), BF16),
            jax.ShapeDtypeStruct((cent, feat), BF16),
        ),
        in_specs=[vm, vm],
        out_specs=(anyw, anyw),
        scratch_shapes=[dma((2,))],
    )(
        pltpu.with_memory_space_constraint(potential, pltpu.VMEM),
        pltpu.with_memory_space_constraint(centre_features, pltpu.VMEM),
    )
    return (potential.T, centre_features)


def solution(mesh):
    return jax.shard_map(
        functools.partial(shards, mesh.shape["mat"], mesh.shape["pts"]),
        mesh=mesh,
        in_specs=(
            P(("mat", "pts"), None, None),
            P(("mat", "pts"), None),
            P("mat", None),
            P(("mat", "pts"), None, None),
            P(("mat", "pts"), None),
            P(("mat", "pts"), None),
            P(), P(), P(), P(), P(), P(), P(), P(),
        ),
        out_specs=(P("mat", "pts"), P("pts", None)),
        check_vma=False,
    )
```

```python
import functools
import math

import jax
import jax.numpy as jnp
from jax import lax
from jax.experimental import pallas as pl
from jax.experimental.pallas import tpu as pltpu
from jax.sharding import PartitionSpec as P

SPLIT = 2
MESH = pl.DeviceIdType.MESH
F32 = jnp.float32
BF16 = jnp.bfloat16
NT_DIMS = (((1,), (1,)), ((), ()))


def silu(v):
    h = 0.5 * v
    return h + h * jnp.tanh(h)


def place(pot, cf, out_pot, out_cf, sem):
    copies = [pltpu.make_async_copy(pot, out_pot, sem.at[0]), pltpu.make_async_copy(cf, out_cf, sem.at[1])]
    for c in copies:
        c.start()
    for c in copies:
        c.wait()


def kernel(
    nm, npts, factor,
    v_hbm, d_hbm, tiles_hbm, dm_hbm, gw_hbm, ids_hbm, scale_hbm, gain_hbm,
    w1_hbm, b1_hbm, w2_hbm, b2_hbm, w3_hbm, b3_hbm,
    out_pot, out_cf,
    tiles, gw, ids, w13, b12, sgb, w2, gain_col, b3_col,
    vbuf, dbuf, vt, oh, dens, pps, panel, cpart, cs_src, cs_in, cz_src, cz_in,
    full, cf_s, cft, acc, psnd, pin, whole, snd, rin, red, zsnd, zin,
    isem, msem, vsem, ag_s, ag_r, fw_r, cs_s, cs_r, cz_s, cz_r, cg_s, cg_r, pr_r, rp_r, rz_s, rz_r,
):
    m = lax.axis_index("mat")
    p = lax.axis_index("pts")
    batches = len(vbuf)
    per_batch, points, tile = vbuf[0].shape
    rows, nb = dm_hbm.shape
    ntile = nb // tile
    feat = dbuf.shape[1]
    ncent = oh.shape[1]
    slab = nb // npts
    piece = rows // SPLIT

    small = [
        pltpu.make_async_copy(a, b, isem.at[i]) for i, (a, b) in enumerate((
            (tiles_hbm, tiles), (ids_hbm, ids), (dm_hbm, panel.at[pl.ds(pl.multiple_of(m * rows, rows), rows)]),
            (gw_hbm, gw), (w2_hbm, w2), (d_hbm, dbuf)))]
    grouped = [
        pltpu.make_async_copy(a, b, msem.at[i]) for a, b, i in (
            (w1_hbm, w13.at[0], 0), (w3_hbm, w13.at[1], 0), (b1_hbm, b12.at[0], 1), (b2_hbm, b12.at[1], 1),
            (scale_hbm, sgb.at[0], 2), (gain_hbm, sgb.at[1], 2), (b3_hbm, sgb.at[2], 2))]

    def vcopy(b, j):
        return pltpu.make_async_copy(v_hbm.at[b, :, pl.ds(j * tile, tile)], vbuf[b].at[j], vsem.at[b])

    barrier = pltpu.get_barrier_semaphore()
    for k in range(1, nm):
        pl.semaphore_signal(barrier, inc=1, device_id={"mat": lax.rem(m + k, nm)}, device_id_type=MESH)
    for k in range(1, npts):
        pl.semaphore_signal(barrier, inc=1, device_id={"pts": lax.rem(p + k, npts)}, device_id_type=MESH)
    for c in small[:3]:
        c.start()
    for j in range(per_batch):
        vcopy(0, j).start()
    pl.semaphore_wait(barrier, npts + nm - 2)

    def remote(src, dst, s, r, **where):
        return pltpu.make_async_remote_copy(
            src_ref=src, dst_ref=dst, send_sem=s, recv_sem=r, device_id=where, device_id_type=MESH
        )

    def at_rows(owner, part):
        return pl.ds(pl.multiple_of(owner * rows + part * piece, piece), piece)

    g = lax.rem(p, SPLIT)
    base = p - g
    near = m + 1 - 2 * lax.rem(m, 2)
    order = [near] + [lax.rem(m + 2 * (k // 2) + lax.rem(m + k, 2) - lax.rem(m, 2) + nm, nm) for k in range(2, nm)]
    ag = []
    for k, to in enumerate(order):
        ag.append(remote(
            dm_hbm.at[pl.ds(pl.multiple_of(g * piece, piece), piece)], panel.at[at_rows(m, g)],
            ag_s, ag_r.at[m], mat=to))
    for c in ag:
        c.start()
    for b in range(1, batches):
        for j in range(per_batch):
            vcopy(b, j).start()
    for c in small[3:] + grouped:
        c.start()
    small[0].wait()

    def part(b, owner, which=slice(None)):
        at = pl.ds(pl.multiple_of(owner * rows, rows), rows)
        q = jnp.dot(panel[at, :], vt.at[b][:, which], preferred_element_type=F32)
        return jnp.sum(q * vt.at[b][at, which].astype(F32), axis=0, keepdims=True)

    def prepare(b):
        held = [tiles[b, j] for j in range(per_batch)]

        def find(t, value, otherwise):
            for j in range(per_batch):
                otherwise = jnp.where(held[j] == t, value(j), otherwise)
            return otherwise

        spot = [find(t, lambda j: j, 0) for t in range(ntile)]
        here = [find(t, lambda j: 1, 0) for t in range(ntile)]
        for t in range(ntile):
            x = vbuf[b][spot[t]]
            if ntile != per_batch:
                x = jnp.where(here[t] == 1, x, jnp.zeros_like(x))
            vt.at[b][t * tile:(t + 1) * tile, :] = x.T

    def mask(b):
        which = lax.broadcasted_iota(jnp.int32, (ncent, points), 0)
        oh[b] = jnp.where(which == ids[b:b + 1, :], 1.0, 0.0).astype(BF16)

    fw = []

    def ahead(k):
        src = order[k]
        return remote(
            dm_hbm.at[pl.ds(0, piece)], panel.at[at_rows(src, g)], ag_s, ag_r.at[src], mat=src)

    def receive(k):
        ahead(k).wait_recv()
        held = panel.at[at_rows(order[k], g)]
        mine = []
        for h in range(1, SPLIT):
            i = k * (SPLIT - 1) + h - 1
            c = remote(held, held, ag_s, fw_r.at[i], pts=base + lax.rem(g + h, SPLIT))
            c.start()
            mine.append(c)
        fw.extend(mine)
        return mine

    for b in range(batches):
        if b == 1:
            small[1].wait()
            small[2].wait()
        pltpu.make_async_copy(vbuf[b], vbuf[b], vsem.at[b]).wait()
        if b:
            dens[b - 1] = part(b - 1, m)
            mask(b - 1)
        prepare(b)
    passing = receive(0)
    for c in small[3:]:
        c.wait()
    pltpu.make_async_copy(w13, w13, msem.at[0]).wait()
    pltpu.make_async_copy(b12, b12, msem.at[1]).wait()
    pltpu.make_async_copy(sgb, sgb, msem.at[2]).wait()
    scale, gain, b3 = sgb.at[0], sgb.at[1], sgb.at[2]
    w1, w3 = w13.at[0], w13.at[1]
    b1, b2 = b12.at[0], b12.at[1]

    def column(row):
        return jnp.broadcast_to(row[...], (128, feat)).T[:, :1]

    scale_col = column(scale)
    gain_col[...] = jnp.broadcast_to(column(gain), gain_col.shape)
    b3_col[...] = jnp.broadcast_to(column(b3), b3_col.shape)
    cpart[...] = jnp.zeros_like(cpart)

    dens[batches - 1] = part(batches - 1, m)
    mask(batches - 1)
    for k in range(nm - 2):
        for c in passing:
            c.wait_recv()
        passing = receive(k + 1)

        def step(i, carry):
            for b in (2 * i, 2 * i + 1):
                dens[b] += part(b, order[k])
            return carry

        lax.fori_loop(0, batches // 2, step, 0)
    for c in passing:
        c.wait_recv()
    for b in range(batches):
        d = dens[b] + part(b, order[nm - 2])
        dens[b] = d
        wf = gw[pl.ds(b, 1), :] * silu(d * scale_col + dbuf[b].astype(F32))
        high = wf.astype(BF16)
        low = (wf - high.astype(F32)).astype(BF16)
        both = lax.dot_general(
            jnp.concatenate([high, low], axis=0), oh[b], NT_DIMS, preferred_element_type=F32)
        cpart[...] += both[:feat] + both[feat:]

    far = sorted(range(1, npts), key=lambda k: -min(k, npts - k))
    fp = feat // npts
    for i in range(npts):
        cs_src[i] = cpart[i * fp:(i + 1) * fp, :]
    for k in far:
        to = lax.rem(p + k, npts)
        remote(cs_src.at[to], cs_in.at[k - 1], cs_s, cs_r, pts=to).start()
    all_cs = remote(cs_in, cs_in, cs_s, cs_r, pts=lax.rem(p + 1, npts))
    all_cs.wait_recv()
    mine = cs_src[p]
    for k in range(1, npts):
        mine = mine + cs_in[k - 1]
    cz_src[...] = mine
    for k in sorted(range(1, nm), key=lambda k: -min(k, nm - k)):
        to = lax.rem(m + k, nm)
        remote(cz_src, cz_in.at[k - 1], cz_s, cz_r, mat=to).start()
    all_cz = remote(cz_in, cz_in, cz_s, cz_r, mat=lax.rem(m + 1, nm))
    all_cz.wait_recv()
    total = mine
    for k in range(1, nm):
        total = total + cz_in[k - 1]
    full[npts - 1] = total
    for k in far:
        remote(full.at[npts - 1], full.at[k - 1], cg_s, cg_r, pts=lax.rem(p + k, npts)).start()
    others = full.at[pl.ds(0, npts - 1)]
    all_cg = remote(others, others, cg_s, cg_r, pts=lax.rem(p + 1, npts))
    all_cg.wait_recv()

    summed = jnp.concatenate([full[lax.rem(p - i - 1 + npts, npts)] for i in range(npts)], axis=0)
    inverse = lax.rsqrt(jnp.mean(summed * summed, axis=0, keepdims=True) + 1e-05)
    normed = (summed * inverse * gain_col[...]).T.astype(BF16)
    one = silu(jnp.dot(normed, w1[...], preferred_element_type=F32) + b1[...]).astype(BF16)
    two = silu(jnp.dot(one, w2[...], preferred_element_type=F32) + b2[...]).astype(BF16)
    cft[...] = (lax.dot_general(w3[...], two, NT_DIMS, preferred_element_type=F32) + b3_col[...]).astype(BF16)

    def spot(u, i):
        return 2 * i + (i + u) % 2 if isinstance(u, int) else 2 * i + lax.rem(i + u, 2)

    pairs = npts // 2
    mid = pairs // 2
    core = lax.rem(p, 2)
    chip = p // 2
    buddy = p + 1 - 2 * core

    for b in range(batches):
        nearest = jnp.dot(cft[...], oh[b], preferred_element_type=F32)
        along = jnp.sum(nearest * dbuf[b].astype(F32), axis=0, keepdims=True)
        pps[b] = gw[pl.ds(b, 1), :] * dens[b] * along * factor

    def side(b, u):
        return jnp.concatenate([
            vt.at[b][pl.ds(pl.multiple_of(spot(u, i) * tile, tile), tile), :] for i in range(mid)], axis=0)

    def quarter(u, w):
        r = 0
        for b in range(batches):
            left = (side(b, u).astype(F32) * pps[b]).astype(BF16)
            r = r + lax.dot_general(left, side(b, w), NT_DIMS, preferred_element_type=F32)
        return r

    def keep(r, first):
        for i in range(mid):
            for q in range(2):
                acc[q, first + i] = r[(2 * i + q) * slab:(2 * i + q + 1) * slab]

    stages = [
        (0, [(spot(0, i), 0) for i in range(mid)]),
        (mid, [(spot(1, i), 0) for i in range(mid)] + [(spot(0, i), 1) for i in range(mid)]),
        (3 * mid, [(spot(1, i), 1) for i in range(mid)]),
    ]

    def pair(n):
        first, entries = stages[n]
        at = pl.ds(first, len(entries))
        return remote(psnd.at[at], pin.at[at], ag_s, pr_r.at[n], pts=buddy)

    def give(n):
        first, entries = stages[n]
        for e in range(first, first + len(entries)):
            psnd[e] = acc[1 - core, e].astype(BF16)
        pair(n).start()

    def plane(to, u):
        return remote(snd.at[to, u], rin.at[u, lax.rem(to - chip - 1 + pairs, pairs)], ag_s, rp_r.at[u], pts=2 * to + core)

    def spread(n):
        first, entries = stages[n]
        pair(n).wait_recv()
        for e, (to, u) in enumerate(entries):
            both = acc[core, first + e] + pin[first + e].astype(F32)
            whole[to, u] = both
            snd[to, u] = both.astype(BF16)
        for to, u in entries:
            @pl.when(to != chip)
            def _():
                plane(to, u).start()


    def turn(n, carry):
        keep(quarter(n // 2, (n + 1) // 2), jnp.where(n == 0, 0, (n + 1) * mid))

        @pl.when(n == 0)
        def _():
            give(0)

        @pl.when(n == 1)
        def _():
            across = jnp.concatenate([acc[q, 2 * mid + i] for i in range(mid) for q in range(2)], axis=0)
            keep(across.T, mid)
            give(1)
            spread(0)

        @pl.when(n == 2)
        def _():
            give(2)
            spread(1)

        return carry

    lax.fori_loop(0, 3, turn, 0)
    cf_s[...] = cft[...].astype(F32).T
    cent = out_cf.shape[0]
    out_cf[...] = cf_s[pl.ds(pl.multiple_of(p * cent, cent), cent), :].astype(BF16)
    spread(2)
    for u in range(2):
        mine = whole[chip, u]
        remote(rin.at[u], rin.at[u], ag_s, rp_r.at[u], pts=buddy).wait_recv()
        for k in range(pairs - 1):
            mine = mine + rin[u, k].astype(F32)
        for i in range(mid):
            to = 2 * i + lax.rem(i + u, 2)
            red[to] = mine[:, i * tile:(i + 1) * tile]
            zsnd[to] = mine[:, i * tile:(i + 1) * tile].astype(BF16)

            @pl.when(to != m)
            def _():
                remote(zsnd.at[to], zin.at[lax.rem(to - m - 1 + nm, nm)], rz_s, rz_r, mat=to).start()
    mine = red[m]
    all_rz = remote(zin, zin, rz_s, rz_r, mat=lax.rem(m + 1, nm))
    all_rz.wait_recv()
    for k in range(nm - 1):
        mine = mine + zin[k].astype(F32)
    out_pot[...] = mine.astype(BF16)

    for c in (all_cs, all_cz, all_cg, all_rz):
        c.wait_send()
    moved = (nm - 1) * SPLIT * piece * nb + (npts + 2 * (pairs - 1)) * slab * (nb // 2)
    sent = vt.at[0, pl.ds(0, moved // points)]
    remote(sent, sent, ag_s, ag_r.at[m], pts=buddy).wait_send()


def shards(
    nm, npts,
    basis_values, tile_ids, density_matrix, descriptors, grid_weights, centre_ids,
    density_scale, norm_gain, w_first, b_first, w_second, b_second, w_third, b_third,
):
    batches, points, orbitals = basis_values.shape
    per_batch = tile_ids.shape[1]
    tile = orbitals // per_batch
    rows, nb = density_matrix.shape
    feat = descriptors.shape[2]
    hid = w_first.shape[1]
    ntile = nb // tile
    cent = 16
    ncent = cent * npts
    slab = nb // npts
    width = nb // nm
    factor = ntile / (per_batch * math.sqrt(points * feat * batches * nm * npts))
    vm = pl.BlockSpec(memory_space=pltpu.VMEM)
    anyw = pl.BlockSpec(memory_space=pl.ANY)
    fp = feat // npts
    dma = pltpu.SemaphoreType.DMA
    nfw = (nm - 1) * (SPLIT - 1)
    potential, centre_features = pl.pallas_call(
        functools.partial(kernel, nm, npts, factor),
        out_shape=(pltpu.VMEM((slab, width), BF16), pltpu.VMEM((cent, feat), BF16)),
        in_specs=[anyw] * 14,
        out_specs=(vm, vm),
        scratch_shapes=[
            pltpu.SMEM((batches, per_batch), jnp.int32),
            pltpu.VMEM((batches, points), F32),
            pltpu.VMEM((batches, points), jnp.int32),
            pltpu.VMEM((2, feat, hid), BF16),
            pltpu.VMEM((2, 1, hid), F32),
            pltpu.VMEM((3, 1, feat), F32),
            pltpu.VMEM((hid, hid), BF16),
            pltpu.VMEM((feat, ncent), F32),
            pltpu.VMEM((feat, ncent), F32),
            [pltpu.VMEM((per_batch, points, tile), BF16) for _ in range(batches)],
            pltpu.VMEM((batches, feat, points), BF16),
            pltpu.VMEM((batches, nb, points), BF16),
            pltpu.VMEM((batches, ncent, points), BF16),
            pltpu.VMEM((batches, 1, points), F32),
            pltpu.VMEM((batches, 1, points), F32),
            pltpu.VMEM((nb, nb), BF16),
            pltpu.VMEM((feat, ncent), F32),
            pltpu.VMEM((npts, fp, ncent), F32),
            pltpu.VMEM((npts - 1, fp, ncent), F32),
            pltpu.VMEM((fp, ncent), F32),
            pltpu.VMEM((nm - 1, fp, ncent), F32),
            pltpu.VMEM((npts, fp, ncent), F32),
            pltpu.VMEM((ncent, feat), F32),
            pltpu.VMEM((feat, ncent), BF16),
            pltpu.VMEM((2, npts, slab, nb // 2), F32),
            pltpu.VMEM((npts, slab, nb // 2), BF16),
            pltpu.VMEM((npts, slab, nb // 2), BF16),
            pltpu.VMEM((npts // 2, 2, slab, nb // 2), F32),
            pltpu.VMEM((npts // 2, 2, slab, nb // 2), BF16),
            pltpu.VMEM((2, npts // 2 - 1, slab, nb // 2), BF16),
            pltpu.VMEM((nm, slab, width), F32),
            pltpu.VMEM((nm, slab, width), BF16),
            pltpu.VMEM((nm - 1, slab, width), BF16),
            dma((6,)), dma((3,)), dma((batches,)),
            dma, dma((nm,)), dma((nfw,)),
            dma, dma, dma, dma, dma, dma,
            dma((3,)), dma((2,)), dma, dma,
        ],
        compiler_params=pltpu.CompilerParams(
            collective_id=0, has_side_effects=True, vmem_limit_bytes=60 * 1024 * 1024
        ),
    )(
        basis_values, descriptors.transpose(0, 2, 1), tile_ids, density_matrix, grid_weights, centre_ids,
        density_scale.reshape(1, -1), norm_gain.reshape(1, -1),
        w_first, b_first.reshape(1, -1), w_second, b_second.reshape(1, -1),
        w_third.T, b_third.reshape(1, -1),
    )
    potential, centre_features = pl.pallas_call(
        place,
        out_shape=(
            jax.ShapeDtypeStruct((slab, width), BF16),
            jax.ShapeDtypeStruct((cent, feat), BF16),
        ),
        in_specs=[vm, vm],
        out_specs=(anyw, anyw),
        scratch_shapes=[dma((2,))],
    )(
        pltpu.with_memory_space_constraint(potential, pltpu.VMEM),
        pltpu.with_memory_space_constraint(centre_features, pltpu.VMEM),
    )
    return (potential.T, centre_features)


def solution(mesh):
    return jax.shard_map(
        functools.partial(shards, mesh.shape["mat"], mesh.shape["pts"]),
        mesh=mesh,
        in_specs=(
            P(("mat", "pts"), None, None),
            P(("mat", "pts"), None),
            P("mat", None),
            P(("mat", "pts"), None, None),
            P(("mat", "pts"), None),
            P(("mat", "pts"), None),
            P(), P(), P(), P(), P(), P(), P(), P(),
        ),
        out_specs=(P("mat", "pts"), P("pts", None)),
        check_vma=False,
    )
```
